256 devices in a mesh: gx: 4 (over y), gy: 16 (over z, core), gz: 4 (over x).
Axes of the slice: x: 4, y: 4, z: 8, core: 2. Of those that a mesh axis runs over, the one named last changes fastest.
Arguments:
- field: bfloat16 [16, 64, 256, 512], P(None, 'gz', 'gy', 'gx'), may hold values from -6 to 6
- fine_taps: float32 [3, 9], replicated, may hold values from 0.1 to 0.6
- coarse_taps: float32 [3, 9], replicated, may hold values from 0.1 to 0.6
- top_kernel: bfloat16 [8, 32, 64, 16384], P('gz', 'gy', 'gx'), may hold values from -4 to 4
Outputs:
- applied: bfloat16 [16, 64, 256, 512], P(None, 'gz', 'gy', 'gx')
The draws below stay inside these ranges and needn't reach their ends.
All inputs are finite; a program needn't handle non-finite values.
Results may differ from the reference program's by a relative error of at most 0.0047.
Values may be sent and summed in bfloat16 or wider, within the bound.
A program may use at most 128 MiB of HBM per device.

```python
import jax
import jax.numpy as jnp
from jax import lax

V = 16
NX = 512
NY = 256
NZ = 64
TOP = 16384


def level_of(stream_key, extent, pieces, least, top_value):
    level, own = 1.0, jax.random.fold_in(stream_key, 6)
    for position, parts in pieces:
        steps = jnp.exp(jax.random.uniform(jax.random.fold_in(own, position), (parts,), jnp.float32, least / len(pieces), top_value / len(pieces)))
        level = level * jnp.repeat(steps, extent[position] // parts).reshape([-1 if axis == position else 1 for axis in range(len(extent))])
    return level


def noise(rng, extent, width, bound, split=(), dtype=jnp.bfloat16):
    factor_of = level_of(rng, extent, split, -0.22, 0.18) if split else 1.0
    result = jax.random.normal(rng, extent, jnp.float32) * width * factor_of
    return jnp.minimum(jnp.maximum(result, -bound), bound).astype(dtype)


def setup_inputs(seed: int = 0) -> dict:
    splits = jax.random.split(jax.random.key(seed), 5)
    field = noise(splits[0], (V, NZ, NY, NX), 1.0, 6.0, ((1, 4), (2, 16), (3, 4)))
    fine_taps = jnp.clip(jax.random.uniform(splits[1], (3, 9), jnp.float32, 0.1, 0.6), 0.1, 0.6)
    coarse_taps = jnp.clip(jax.random.uniform(splits[2], (3, 9), jnp.float32, 0.1, 0.6), 0.1, 0.6)
    top_kernel = noise(splits[3], (NZ // 8, NY // 8, NX // 8, TOP), (32.0 / TOP ** 0.5), 4.0, ((0, 4), (1, 16), (2, 4)))
    return dict(field=field, fine_taps=fine_taps, coarse_taps=coarse_taps, top_kernel=top_kernel)


def conv_axis(values, kernel_row, along):
    length = values.shape[along]
    widths = [(0, 0)] * values.ndim
    widths[along] = (4, 4)
    padded = jnp.pad(values, widths)
    total = kernel_row[0] * lax.slice_in_dim(padded, 0, length, axis=along)
    for offset in range(1, 9):
        total = total + kernel_row[offset] * lax.slice_in_dim(padded, offset, offset + length, axis=along)
    return total


def separable(values, kernel):
    values = conv_axis(values, kernel[2], 2)
    values = conv_axis(values, kernel[1], 1)
    return conv_axis(values, kernel[0], 0)


def restrict(values, factor):
    depth, rows, cols = values.shape
    return values.reshape(depth // factor, factor, rows // factor, factor, cols // factor, factor).mean(axis=(1, 3, 5))


def prolong(values, factor):
    values = jnp.repeat(values, factor, axis=0)
    values = jnp.repeat(values, factor, axis=1)
    return jnp.repeat(values, factor, axis=2)


def reference(field, fine_taps, coarse_taps, top_kernel):
    def top_input(cells):
        coarse_cells = restrict(cells.astype(jnp.float32), 2)
        return restrict(coarse_cells, 4).astype(jnp.bfloat16)

    top_in = lax.map(top_input, field)
    kernel_rows = top_kernel.reshape(-1, top_kernel.shape[3])
    flat_in = top_in.reshape(top_in.shape[0], -1)
    top_part = lax.dot_general(flat_in, kernel_rows, (((1,), (1,)), ((), ())), preferred_element_type=jnp.float32).reshape(top_in.shape)

    def apply_one(inputs_pair):
        cells, top_piece = inputs_pair
        cells = cells.astype(jnp.float32)
        fine_part = separable(cells, fine_taps)
        coarse_cells = restrict(cells, 2)
        coarse_total = separable(coarse_cells, coarse_taps) + prolong(top_piece, 4)
        return (fine_part + prolong(coarse_total, 2)).astype(jnp.bfloat16)

    return lax.map(apply_one, (field, top_part))
```

```python
import functools

import jax
import jax.numpy as jnp
from jax import lax
from jax.experimental import pallas as pl
from jax.experimental.pallas import tpu as pltpu
from jax.sharding import PartitionSpec as P

F32 = jnp.float32
BF16 = jnp.bfloat16
MESH = pl.DeviceIdType.MESH
NGX, NGY, NGZ = 4, 16, 4
NCH = 2
VCH = 16 // NCH
PCH = 8 // NCH
SIDES = [(1, 0), (-1, 0), (0, 1), (0, -1), (1, 1), (1, -1), (-1, 1), (-1, -1)]


def iota(shape, dim):
    return lax.broadcasted_iota(jnp.int32, shape, dim)


def nn(a, b):
    return lax.dot_general(a, b, (((1,), (0,)), ((), ())), preferred_element_type=F32)


def nt(a, b):
    return lax.dot_general(a, b, (((1,), (1,)), ((), ())), preferred_element_type=F32)


def tn(a, b):
    return lax.dot_general(a, b, (((0,), (0,)), ((), ())), preferred_element_type=F32)


def hi_lo(w):
    hi = w.astype(BF16)
    return hi, (w - hi.astype(F32)).astype(BF16)


def taps_at(taps_ref, row, offset):
    value = jnp.zeros(offset.shape, F32)
    for k in range(9):
        value = jnp.where(offset == k, taps_ref[row, k], value)
    return value


def kernel(
    field, fine_taps, coarse_taps, top, out,
    fld, halo, strips, cl, ch, tt, edge_out, edge_in, base, res,
    wf, wc, xw, xh, gsel, rx, perm, kv, kp, gath, tile_in, psum, acc, prol,
    fs, fr, cs, cr, es, er, s1s, s1r, s2s, s2r, s3s, s3r, lsem, osem,
):
    gx, gy, gz = lax.axis_index("gx"), lax.axis_index("gy"), lax.axis_index("gz")

    def dev(dx, dy, dz):
        return (
            lax.rem(gx + (dx + NGX), NGX),
            lax.rem(gy + (dy + NGY), NGY),
            lax.rem(gz + (dz + NGZ), NGZ),
        )

    def remote(src, dst, ssem, rsem, to):
        return pltpu.make_async_remote_copy(
            src_ref=src, dst_ref=dst, send_sem=ssem, recv_sem=rsem, device_id=to, device_id_type=MESH
        )

    load_field = pltpu.make_async_copy(field, fld, lsem.at[0])
    load_top = pltpu.make_async_copy(top, kv, lsem.at[1])
    load_field.start()
    load_top.start()

    barrier = pltpu.get_barrier_semaphore()
    partners = [(i, 0, 0) for i in range(1, NGX)] + [(0, i, 0) for i in range(1, NGY)]
    partners += [(0, 0, i) for i in range(1, NGZ)] + [(0, dy, dz) for dz, dy in SIDES[4:]]
    for d in partners:
        pl.semaphore_signal(barrier, inc=1, device_id=dev(*d), device_id_type=MESH)

    r, c = iota((192, 256), 0), iota((192, 256), 1)
    z, y = c >> 4, c & 15
    strip_z, strip_y = (r & 63) >> 2, (r & 3) + jnp.where(r >= 64, 12, 0)
    q = r - 128
    cz, cy = ((q >> 5) << 2) + ((q >> 2) & 3), (((q >> 4) & 1) << 2) + (q & 3)
    is_strip = (z == strip_z) & (y == strip_y)
    is_mean = ((z >> 1) == cz) & ((y >> 1) == cy)
    gsel[...] = jnp.where(
        r < 128, jnp.where(is_strip, 1.0, 0.0), jnp.where(is_mean, 0.25, 0.0)
    ).astype(BF16)
    k, n = iota((512, 128), 0), iota((512, 128), 1)
    rx[...] = jnp.where(((k >> 8) == (n >> 6)) & (((k & 127) >> 1) == (n & 63)), 0.5, 0.0).astype(BF16)

    load_field.wait()
    r, c = iota((32, 256), 0), iota((32, 256), 1)
    rows = jnp.where(((r & 15) == (c >> 4)) & (((c & 15) >> 3) == (r >> 4)), 1.0, 0.0).astype(BF16)
    for zt in range(2):
        total = fld[:, pl.ds(zt * 128, 16), :].astype(F32)
        for i in range(1, 8):
            total = total + fld[:, pl.ds(zt * 128 + i * 16, 16), :].astype(F32)
        total = total.reshape(256, 128)
        hi, lo = hi_lo(total)
        lo2 = (total - hi.astype(F32) - lo.astype(F32)).astype(BF16)
        both = nn(rows, hi) + nn(rows, lo) + nn(rows, lo2)
        for yt in range(2):
            psum[:, pl.ds((zt * 2 + yt) * 128, 128)] = both[yt * 16 : yt * 16 + 16]
    k, n = iota((512, 128), 0), iota((512, 128), 1)
    spot = lax.rem(gz, 2) * 64 + ((k >> 7) << 4) + ((k & 127) >> 3)
    place = jnp.where(n == spot, 1.0 / 512.0, 0.0).astype(BF16)
    sums = psum[...]
    hi, lo = hi_lo(sums)
    lo2 = (sums - hi.astype(F32) - lo.astype(F32)).astype(BF16)
    tile_in[gz] = (nn(hi, place) + nn(lo, place) + nn(lo2, place)).astype(BF16)

    pl.semaphore_wait(barrier, len(partners))

    stage1 = []
    for d in range(1, NGZ):
        cp = remote(tile_in.at[gz], tile_in.at[gz], s1s.at[d - 1], s1r.at[d - 1], dev(0, 0, d))
        cp.start()
        stage1.append(cp)

    def fine_copy(h, i):
        dz, dy = SIDES[i]
        vs = pl.ds(h * VCH, VCH)
        if dy == 0:
            src = fld.at[vs, pl.ds(192 if dz > 0 else 0, 64)]
            dst = halo.at[vs, pl.ds(0 if dz > 0 else 64, 64)]
        elif dz == 0:
            src = strips.at[1 if dy > 0 else 0, vs]
            dst = halo.at[vs, pl.ds(128 if dy > 0 else 192, 64)]
        else:
            src = strips.at[1 if dy > 0 else 0, vs, pl.ds(48 if dz > 0 else 0, 16)]
            dst = halo.at[vs, pl.ds(256 + (0 if dz > 0 else 32) + (0 if dy > 0 else 16), 16)]
        return remote(src, dst, fs.at[h, i], fr.at[h, i], dev(0, dy, dz))

    def coarse_copy(i):
        dz, dy = SIDES[i]
        if dy == 0:
            src, dst = cl.at[:, 1 if dz > 0 else 0], ch.at[:, pl.ds(0 if dz > 0 else 2, 2)]
        elif dz == 0:
            src, dst = cl.at[:, :, 1 if dy > 0 else 0], ch.at[:, pl.ds(4 if dy > 0 else 6, 2)]
        else:
            src = cl.at[:, 1 if dz > 0 else 0, 1 if dy > 0 else 0]
            dst = ch.at[:, 8 + (0 if dz > 0 else 2) + (0 if dy > 0 else 1)]
        return remote(src, dst, cs.at[i], cr.at[i], dev(0, dy, dz))

    fine = [[fine_copy(h, i) for i in range(8)] for h in range(NCH)]
    coarse = [coarse_copy(i) for i in range(8)]
    for h in range(NCH):
        fine[h][0].start()
        fine[h][1].start()

    def cut(p, carry):
        pair = jnp.concatenate([fld[2 * p], fld[2 * p + 1]], axis=1)
        got = nn(gsel[...], pair)
        for v in range(2):
            for side in range(2):
                strips[side, 2 * p + v] = got[side * 64 : side * 64 + 64, v * 128 : v * 128 + 128].astype(BF16)
        means = got[128:192]
        hi, lo = hi_lo(means)
        both = jnp.concatenate([hi[:, :128], lo[:, :128], hi[:, 128:], lo[:, 128:]], axis=1)
        cl[p] = nn(both, rx[...]).astype(BF16).reshape(2, 2, 16, 128)
        return carry

    lax.fori_loop(0, 8, cut, 0)
    for i in range(2, 8):
        fine[0][i].start()
    for i in range(8):
        coarse[i].start()
    for h in range(1, NCH):
        for i in range(2, 8):
            fine[h][i].start()

    for cp in stage1:
        cp.wait()
    for half in range(2):
        gath[gx, gy, half] = tile_in[2 * half] + tile_in[2 * half + 1]
    stage2 = []
    for d in range(1, NGY):
        cp = remote(gath.at[gx, gy], gath.at[gx, gy], s2s.at[d - 1], s2r.at[d - 1], dev(0, d, 0))
        cp.start()
        stage2.append(cp)

    zmin, zmax = jnp.where(gz > 0, -99, 0), jnp.where(gz < NGZ - 1, 99, 0)
    ymin, ymax = jnp.where(gy > 0, -99, 0), jnp.where(gy < NGY - 1, 99, 0)

    def zy_weights(taps_ref, zi, yi, zo, yo, side):
        ok = (zi >= zmin) & (yi >= ymin) & (zi < zmax + side) & (yi < ymax + side)
        w = taps_at(taps_ref, 0, zi - zo + 4) * taps_at(taps_ref, 1, yi - yo + 4)
        return hi_lo(jnp.where(ok, w, 0.0))

    o, c = iota((256, 256), 0), iota((256, 256), 1)
    hi, lo = zy_weights(fine_taps, c >> 4, c & 15, o >> 4, o & 15, 16)
    wf[0, :, pl.ds(0, 256)] = hi
    wf[1, :, pl.ds(0, 256)] = lo
    o, c = iota((256, 320), 0), iota((256, 320), 1)
    z4, y4, q = (c >> 2) & 3, c & 3, (c >> 4) & 3
    zi = jnp.where(
        c < 64, (c >> 4) - 4, jnp.where(c < 128, (c >> 4) + 12, jnp.where(c < 256, (c & 63) >> 2, jnp.where(q < 2, z4 - 4, z4 + 16)))
    )
    yi = jnp.where(
        c < 128, c & 15, jnp.where(c < 192, y4 - 4, jnp.where(c < 256, y4 + 16, jnp.where((q & 1) == 0, y4 - 4, y4 + 16)))
    )
    hi, lo = zy_weights(fine_taps, zi, yi, o >> 4, o & 15, 16)
    wf[0, :, pl.ds(256, 320)] = hi
    wf[1, :, pl.ds(256, 320)] = lo
    o, c = iota((256, 256), 0), iota((256, 256), 1)
    z4, y4, q = (c >> 2) & 3, c & 3, c >> 4
    first = (q & 1) * 4
    zi = jnp.where(
        q < 4, ((q >> 1) << 2) + z4,
        jnp.where(q < 6, z4 - 4, jnp.where(q < 8, z4 + 8, jnp.where(q < 12, first + z4, jnp.where(q < 14, z4 - 4, z4 + 8)))),
    )
    yi = jnp.where(
        q < 8, first + y4,
        jnp.where(q < 10, y4 - 4, jnp.where(q < 12, y4 + 8, jnp.where((q & 1) == 0, y4 - 4, y4 + 8))),
    )
    hi, lo = zy_weights(coarse_taps, zi, yi, o >> 5, (o & 15) >> 1, 8)
    wc[0] = hi
    wc[1] = lo

    k, n = iota((384, 256), 0), iota((384, 256), 1)
    xo, v = n & 127, n >> 7
    w = jnp.where(
        k < 256,
        jnp.where((k >> 7) == v, taps_at(fine_taps, 2, (k & 127) - xo + 4), 0.0),
        jnp.where(((k >> 6) & 1) == v, taps_at(coarse_taps, 2, (k & 63) - (xo >> 1) + 4), 0.0),
    )
    hi, lo = hi_lo(w)
    xw[0] = hi
    xw[1] = lo
    r, n = iota((32, 256), 0), iota((32, 256), 1)
    xo, v, e = n & 127, n >> 7, r & 3
    right = r >= 16
    w = jnp.where(
        (r & 8) == 0,
        taps_at(fine_taps, 2, e + jnp.where(right, 128, -4) - xo + 4),
        taps_at(coarse_taps, 2, e + jnp.where(right, 64, -4) - (xo >> 1) + 4),
    )
    there = jnp.where(right, jnp.where(gx < NGX - 1, 1, 0), jnp.where(gx > 0, 1, 0)) == 1
    hi, lo = hi_lo(jnp.where(there & (((r >> 2) & 1) == v), w, 0.0))
    xh[pl.ds(0, 32)] = hi
    xh[pl.ds(32, 32)] = lo

    for cp in stage2:
        cp.wait()
    stage3 = []
    for d in range(1, NGX):
        cp = remote(gath.at[gx], gath.at[gx], s3s.at[d - 1], s3r.at[d - 1], dev(d, 0, 0))
        cp.start()
        stage3.append(cp)

    load_top.wait()
    k, n = iota((512, 512), 0), iota((512, 512), 1)
    target = (((k >> 4) & 3) << 7) + ((k >> 7) << 5) + (((k >> 6) & 1) << 4) + (k & 15)
    perm[...] = jnp.where(n == target, 1.0, 0.0).astype(BF16)

    def reorder(g, carry):
        parts = []
        for half in range(2):
            pieces = [
                kv[:, pl.ds(pl.multiple_of(((half * 4 + z4) * 16 + g) * 128, 128), 128)] for z4 in range(4)
            ]
            parts.append(jnp.concatenate(pieces, axis=1))
        got = nn(jnp.concatenate(parts, axis=0), perm[...]).astype(BF16)
        for half in range(2):
            for x in range(4):
                kp[x, g, :, pl.ds(half * 128, 128)] = got[half * 64 : half * 64 + 64, x * 128 : x * 128 + 128]
        return carry

    lax.fori_loop(0, NGY, reorder, 0)

    r, c = iota((32, 384), 0), iota((32, 384), 1)
    t, e, right = (r >> 2) & 3, r & 3, r >= 16
    spot = jnp.where(
        t < 2, t * 128 + jnp.where(right, 124, 0), 256 + (t & 1) * 64 + jnp.where(right, 60, 0)
    )
    pick = jnp.where(c == spot + e, 1.0, 0.0).astype(BF16)

    def zy_pass(p, carry):
        pair = jnp.concatenate([fld[2 * p], fld[2 * p + 1]], axis=1)
        near = jnp.concatenate([halo[2 * p], halo[2 * p + 1]], axis=1)
        got = (
            nn(wf[0, :, pl.ds(0, 256)], pair) + nn(wf[0, :, pl.ds(256, 320)], near)
            + nn(wf[1, :, pl.ds(0, 256)], pair) + nn(wf[1, :, pl.ds(256, 320)], near)
        )
        cells = jnp.concatenate([cl[p].reshape(64, 128), ch[p].reshape(192, 128)], axis=0)
        got_coarse = nn(wc[0], cells) + nn(wc[1], cells)
        both = jnp.concatenate([got.astype(BF16), got_coarse.astype(BF16)], axis=1)
        tt[p] = both
        ends = nt(pick, both).astype(BF16)
        edge_out[0, p] = ends[:16]
        edge_out[1, p] = ends[16:]
        return carry

    edges = []
    for cp in coarse:
        cp.wait()
    for h in range(NCH):
        for cp in fine[h]:
            cp.wait()
        lax.fori_loop(h * PCH, (h + 1) * PCH, zy_pass, 0)
        ps = pl.ds(h * PCH, PCH)
        left = remote(edge_out.at[0, ps], edge_in.at[1, ps], es.at[h, 0], er.at[h, 0], dev(-1, 0, 0))
        right = remote(edge_out.at[1, ps], edge_in.at[0, ps], es.at[h, 1], er.at[h, 1], dev(1, 0, 0))
        left.start()
        right.start()
        edges.append((left, right))

    def x_pass(p, carry):
        both = tt[p]
        ends = jnp.concatenate([edge_in[0, p], edge_in[1, p]], axis=0)
        base[p] = nn(both, xw[0]) + nn(both, xw[1]) + tn(jnp.concatenate([ends, ends], axis=0), xh[...])
        return carry

    for h in range(NCH):
        for cp in edges[h]:
            cp.wait()
        lax.fori_loop(h * PCH, (h + 1) * PCH, x_pass, 0)

    def gather_dot(x):
        def add(g, total):
            block = jnp.concatenate([gath[x, g, 0], gath[x, g, 1]], axis=1)
            return total + nt(kp[x, g], block)

        acc[...] = acc[...] + lax.fori_loop(0, NGY, add, jnp.zeros((64, 16), F32))

    acc[...] = jnp.zeros((64, 16), F32)
    gather_dot(gx)
    for d in range(1, NGX):
        stage3[d - 1].wait()
        gather_dot(lax.rem(gx + (NGX - d), NGX))

    k, n = iota((64, 512), 0), iota((64, 512), 1)
    spread = jnp.where(k == ((n >> 7) << 4) + ((n & 127) >> 3), 1.0, 0.0).astype(BF16)
    sums = acc[...]
    hi, lo = hi_lo(sums)
    lo2 = (sums - hi.astype(F32) - lo.astype(F32)).astype(BF16)
    prol[...] = tn(hi, spread) + tn(lo, spread) + tn(lo2, spread)

    for p in range(8):
        for v in range(2):
            for zt in range(2):
                for yt in range(2):
                    row = prol[pl.ds(2 * p + v, 1), pl.ds((zt * 2 + yt) * 128, 128)]
                    block = jnp.broadcast_to(row, (8, 128))
                    for i in range(8):
                        rows = pl.ds((zt * 8 + i) * 16 + yt * 8, 8)
                        base[p, rows, pl.ds(v * 128, 128)] = base[p, rows, pl.ds(v * 128, 128)] + block

    def finish(p, carry):
        for v in range(2):
            res[2 * p + v] = base[p, :, pl.ds(v * 128, 128)].astype(BF16)
        return carry

    lax.fori_loop(0, 8, finish, 0)
    store = pltpu.make_async_copy(res, out, osem.at[0])
    store.start()
    store.wait()


def shards(field, fine_taps, coarse_taps, top_kernel):
    vm = pltpu.VMEM
    dma = pltpu.SemaphoreType.DMA
    smem = pl.BlockSpec(memory_space=pltpu.SMEM)
    hbm = pl.BlockSpec(memory_space=pl.ANY)
    out = pl.pallas_call(
        kernel,
        name="covariance",
        out_shape=jax.ShapeDtypeStruct((16, 256, 128), BF16),
        in_specs=[hbm, smem, smem, hbm],
        out_specs=hbm,
        scratch_shapes=[
            vm((16, 256, 128), BF16),
            vm((16, 320, 128), BF16),
            vm((2, 16, 64, 128), BF16),
            vm((8, 2, 2, 16, 128), BF16),
            vm((8, 12, 16, 128), BF16),
            vm((8, 256, 384), BF16),
            vm((2, 8, 16, 256), BF16),
            vm((2, 8, 16, 256), BF16),
            vm((8, 256, 256), F32),
            vm((16, 256, 128), BF16),
            vm((2, 256, 576), BF16),
            vm((2, 256, 256), BF16),
            vm((2, 384, 256), BF16),
            vm((64, 256), BF16),
            vm((192, 256), BF16),
            vm((512, 128), BF16),
            vm((512, 512), BF16),
            vm((64, 16384), BF16),
            vm((4, 16, 64, 256), BF16),
            vm((4, 16, 2, 16, 128), BF16),
            vm((4, 16, 128), BF16),
            vm((16, 512), F32),
            vm((64, 16), F32),
            vm((16, 512), F32),
            dma((NCH, 8)), dma((NCH, 8)),
            dma((8,)), dma((8,)),
            dma((NCH, 2)), dma((NCH, 2)),
            dma((3,)), dma((3,)),
            dma((15,)), dma((15,)),
            dma((3,)), dma((3,)),
            dma((2,)), dma((1,)),
        ],
        compiler_params=pltpu.CompilerParams(
            collective_id=1, has_side_effects=True, vmem_limit_bytes=40 << 20
        ),
    )(field.reshape(16, 256, 128), fine_taps, coarse_taps, top_kernel.reshape(64, 16384))
    return out.reshape(field.shape)


def solution(mesh):
    return jax.shard_map(
        shards,
        mesh=mesh,
        in_specs=(P(None, "gz", "gy", "gx"), P(), P(), P("gz", "gy", "gx", None)),
        out_specs=P(None, "gz", "gy", "gx"),
        check_vma=False,
    )
```

```python
import functools

import jax
import jax.numpy as jnp
from jax import lax
from jax.experimental import pallas as pl
from jax.experimental.pallas import tpu as pltpu
from jax.sharding import PartitionSpec as P

F32 = jnp.float32
BF16 = jnp.bfloat16
MESH = pl.DeviceIdType.MESH
NGX, NGY, NGZ = 4, 16, 4
NCH = 2
VCH = 16 // NCH
PCH = 8 // NCH
SIDES = [(1, 0), (-1, 0), (0, 1), (0, -1), (1, 1), (1, -1), (-1, 1), (-1, -1)]


def iota(shape, dim):
    return lax.broadcasted_iota(jnp.int32, shape, dim)


def nn(a, b):
    return lax.dot_general(a, b, (((1,), (0,)), ((), ())), preferred_element_type=F32)


def nt(a, b):
    return lax.dot_general(a, b, (((1,), (1,)), ((), ())), preferred_element_type=F32)


def tn(a, b):
    return lax.dot_general(a, b, (((0,), (0,)), ((), ())), preferred_element_type=F32)


def hi_lo(w):
    hi = w.astype(BF16)
    return hi, (w - hi.astype(F32)).astype(BF16)


def taps_at(taps_ref, row, offset):
    value = jnp.zeros(offset.shape, F32)
    for k in range(9):
        value = jnp.where(offset == k, taps_ref[row, k], value)
    return value


def kernel(
    field, fine_hbm, coarse_hbm, top, out,
    fine_taps, coarse_taps,
    fld, halo, strips, cl, ch, tt, edge_out, edge_in, base, res,
    wf, wc, xw, xh, gsel, rx, perm, kv, kp, gath, tile_in, psum, acc, prol,
    fs, fr, cs, cr, es, er, s1s, s1r, s2s, s2r, s3s, s3r, lsem, osem,
):
    gx, gy, gz = lax.axis_index("gx"), lax.axis_index("gy"), lax.axis_index("gz")

    def dev(dx, dy, dz):
        return (
            lax.rem(gx + (dx + NGX), NGX),
            lax.rem(gy + (dy + NGY), NGY),
            lax.rem(gz + (dz + NGZ), NGZ),
        )

    def remote(src, dst, ssem, rsem, to):
        return pltpu.make_async_remote_copy(
            src_ref=src, dst_ref=dst, send_sem=ssem, recv_sem=rsem, device_id=to, device_id_type=MESH
        )

    load_field = pltpu.make_async_copy(field, fld, lsem.at[0])
    load_top = pltpu.make_async_copy(top, kv, lsem.at[1])
    load_fine = pltpu.make_async_copy(fine_hbm, fine_taps, lsem.at[2])
    load_coarse = pltpu.make_async_copy(coarse_hbm, coarse_taps, lsem.at[3])
    load_field.start()
    load_fine.start()
    load_coarse.start()
    load_top.start()

    barrier = pltpu.get_barrier_semaphore()
    partners = [(i, 0, 0) for i in range(1, NGX)] + [(0, i, 0) for i in range(1, NGY)]
    partners += [(0, 0, i) for i in range(1, NGZ)] + [(0, dy, dz) for dz, dy in SIDES[4:]]
    for d in partners:
        pl.semaphore_signal(barrier, inc=1, device_id=dev(*d), device_id_type=MESH)

    r, c = iota((192, 256), 0), iota((192, 256), 1)
    z, y = c >> 4, c & 15
    strip_z, strip_y = (r & 63) >> 2, (r & 3) + jnp.where(r >= 64, 12, 0)
    q = r - 128
    cz, cy = ((q >> 5) << 2) + ((q >> 2) & 3), (((q >> 4) & 1) << 2) + (q & 3)
    is_strip = (z == strip_z) & (y == strip_y)
    is_mean = ((z >> 1) == cz) & ((y >> 1) == cy)
    gsel[...] = jnp.where(
        r < 128, jnp.where(is_strip, 1.0, 0.0), jnp.where(is_mean, 0.25, 0.0)
    ).astype(BF16)
    k, n = iota((512, 128), 0), iota((512, 128), 1)
    rx[...] = jnp.where(((k >> 8) == (n >> 6)) & (((k & 127) >> 1) == (n & 63)), 0.5, 0.0).astype(BF16)

    load_field.wait()
    r, c = iota((32, 256), 0), iota((32, 256), 1)
    rows = jnp.where(((r & 15) == (c >> 4)) & (((c & 15) >> 3) == (r >> 4)), 1.0, 0.0).astype(BF16)
    for zt in range(2):
        total = fld[:, pl.ds(zt * 128, 16), :].astype(F32)
        for i in range(1, 8):
            total = total + fld[:, pl.ds(zt * 128 + i * 16, 16), :].astype(F32)
        total = total.reshape(256, 128)
        hi, lo = hi_lo(total)
        lo2 = (total - hi.astype(F32) - lo.astype(F32)).astype(BF16)
        both = nn(rows, hi) + nn(rows, lo) + nn(rows, lo2)
        for yt in range(2):
            psum[:, pl.ds((zt * 2 + yt) * 128, 128)] = both[yt * 16 : yt * 16 + 16]
    k, n = iota((512, 128), 0), iota((512, 128), 1)
    spot = lax.rem(gz, 2) * 64 + ((k >> 7) << 4) + ((k & 127) >> 3)
    place = jnp.where(n == spot, 1.0 / 512.0, 0.0).astype(BF16)
    sums = psum[...]
    hi, lo = hi_lo(sums)
    lo2 = (sums - hi.astype(F32) - lo.astype(F32)).astype(BF16)
    tile_in[gz] = (nn(hi, place) + nn(lo, place) + nn(lo2, place)).astype(BF16)

    pl.semaphore_wait(barrier, len(partners))

    stage1 = []
    for d in range(1, NGZ):
        cp = remote(tile_in.at[gz], tile_in.at[gz], s1s.at[d - 1], s1r.at[d - 1], dev(0, 0, d))
        cp.start()
        stage1.append(cp)

    def fine_copy(h, i):
        dz, dy = SIDES[i]
        vs = pl.ds(h * VCH, VCH)
        if dy == 0:
            src = fld.at[vs, pl.ds(192 if dz > 0 else 0, 64)]
            dst = halo.at[vs, pl.ds(0 if dz > 0 else 64, 64)]
        elif dz == 0:
            src = strips.at[1 if dy > 0 else 0, vs]
            dst = halo.at[vs, pl.ds(128 if dy > 0 else 192, 64)]
        else:
            src = strips.at[1 if dy > 0 else 0, vs, pl.ds(48 if dz > 0 else 0, 16)]
            dst = halo.at[vs, pl.ds(256 + (0 if dz > 0 else 32) + (0 if dy > 0 else 16), 16)]
        return remote(src, dst, fs.at[h, i], fr.at[h, i], dev(0, dy, dz))

    def coarse_copy(i):
        dz, dy = SIDES[i]
        if dy == 0:
            src, dst = cl.at[:, 1 if dz > 0 else 0], ch.at[:, pl.ds(0 if dz > 0 else 2, 2)]
        elif dz == 0:
            src, dst = cl.at[:, :, 1 if dy > 0 else 0], ch.at[:, pl.ds(4 if dy > 0 else 6, 2)]
        else:
            src = cl.at[:, 1 if dz > 0 else 0, 1 if dy > 0 else 0]
            dst = ch.at[:, 8 + (0 if dz > 0 else 2) + (0 if dy > 0 else 1)]
        return remote(src, dst, cs.at[i], cr.at[i], dev(0, dy, dz))

    fine = [[fine_copy(h, i) for i in range(8)] for h in range(NCH)]
    coarse = [coarse_copy(i) for i in range(8)]
    for h in range(NCH):
        fine[h][0].start()
        fine[h][1].start()

    def cut(p, carry):
        pair = jnp.concatenate([fld[2 * p], fld[2 * p + 1]], axis=1)
        got = nn(gsel[...], pair)
        for v in range(2):
            for side in range(2):
                strips[side, 2 * p + v] = got[side * 64 : side * 64 + 64, v * 128 : v * 128 + 128].astype(BF16)
        means = got[128:192]
        hi, lo = hi_lo(means)
        both = jnp.concatenate([hi[:, :128], lo[:, :128], hi[:, 128:], lo[:, 128:]], axis=1)
        cl[p] = nn(both, rx[...]).astype(BF16).reshape(2, 2, 16, 128)
        return carry

    lax.fori_loop(0, 8, cut, 0)
    for i in range(2, 8):
        fine[0][i].start()
    for i in range(8):
        coarse[i].start()
    for h in range(1, NCH):
        for i in range(2, 8):
            fine[h][i].start()

    for cp in stage1:
        cp.wait()
    for half in range(2):
        gath[gx, gy, half] = tile_in[2 * half] + tile_in[2 * half + 1]
    stage2 = []
    for d in range(1, NGY):
        cp = remote(gath.at[gx, gy], gath.at[gx, gy], s2s.at[d - 1], s2r.at[d - 1], dev(0, d, 0))
        cp.start()
        stage2.append(cp)

    load_fine.wait()
    load_coarse.wait()
    zmin, zmax = jnp.where(gz > 0, -99, 0), jnp.where(gz < NGZ - 1, 99, 0)
    ymin, ymax = jnp.where(gy > 0, -99, 0), jnp.where(gy < NGY - 1, 99, 0)

    def zy_weights(taps_ref, zi, yi, zo, yo, side):
        ok = (zi >= zmin) & (yi >= ymin) & (zi < zmax + side) & (yi < ymax + side)
        w = taps_at(taps_ref, 0, zi - zo + 4) * taps_at(taps_ref, 1, yi - yo + 4)
        return hi_lo(jnp.where(ok, w, 0.0))

    o, c = iota((256, 256), 0), iota((256, 256), 1)
    hi, lo = zy_weights(fine_taps, c >> 4, c & 15, o >> 4, o & 15, 16)
    wf[0, :, pl.ds(0, 256)] = hi
    wf[1, :, pl.ds(0, 256)] = lo
    o, c = iota((256, 320), 0), iota((256, 320), 1)
    z4, y4, q = (c >> 2) & 3, c & 3, (c >> 4) & 3
    zi = jnp.where(
        c < 64, (c >> 4) - 4, jnp.where(c < 128, (c >> 4) + 12, jnp.where(c < 256, (c & 63) >> 2, jnp.where(q < 2, z4 - 4, z4 + 16)))
    )
    yi = jnp.where(
        c < 128, c & 15, jnp.where(c < 192, y4 - 4, jnp.where(c < 256, y4 + 16, jnp.where((q & 1) == 0, y4 - 4, y4 + 16)))
    )
    hi, lo = zy_weights(fine_taps, zi, yi, o >> 4, o & 15, 16)
    wf[0, :, pl.ds(256, 320)] = hi
    wf[1, :, pl.ds(256, 320)] = lo
    o, c = iota((256, 256), 0), iota((256, 256), 1)
    z4, y4, q = (c >> 2) & 3, c & 3, c >> 4
    first = (q & 1) * 4
    zi = jnp.where(
        q < 4, ((q >> 1) << 2) + z4,
        jnp.where(q < 6, z4 - 4, jnp.where(q < 8, z4 + 8, jnp.where(q < 12, first + z4, jnp.where(q < 14, z4 - 4, z4 + 8)))),
    )
    yi = jnp.where(
        q < 8, first + y4,
        jnp.where(q < 10, y4 - 4, jnp.where(q < 12, y4 + 8, jnp.where((q & 1) == 0, y4 - 4, y4 + 8))),
    )
    hi, lo = zy_weights(coarse_taps, zi, yi, o >> 5, (o & 15) >> 1, 8)
    wc[0] = hi
    wc[1] = lo

    k, n = iota((384, 256), 0), iota((384, 256), 1)
    xo, v = n & 127, n >> 7
    w = jnp.where(
        k < 256,
        jnp.where((k >> 7) == v, taps_at(fine_taps, 2, (k & 127) - xo + 4), 0.0),
        jnp.where(((k >> 6) & 1) == v, taps_at(coarse_taps, 2, (k & 63) - (xo >> 1) + 4), 0.0),
    )
    hi, lo = hi_lo(w)
    xw[0] = hi
    xw[1] = lo
    r, n = iota((32, 256), 0), iota((32, 256), 1)
    xo, v, e = n & 127, n >> 7, r & 3
    right = r >= 16
    w = jnp.where(
        (r & 8) == 0,
        taps_at(fine_taps, 2, e + jnp.where(right, 128, -4) - xo + 4),
        taps_at(coarse_taps, 2, e + jnp.where(right, 64, -4) - (xo >> 1) + 4),
    )
    there = jnp.where(right, jnp.where(gx < NGX - 1, 1, 0), jnp.where(gx > 0, 1, 0)) == 1
    hi, lo = hi_lo(jnp.where(there & (((r >> 2) & 1) == v), w, 0.0))
    xh[pl.ds(0, 32)] = hi
    xh[pl.ds(32, 32)] = lo

    for cp in stage2:
        cp.wait()
    stage3 = []
    for d in range(1, NGX):
        cp = remote(gath.at[gx], gath.at[gx], s3s.at[d - 1], s3r.at[d - 1], dev(d, 0, 0))
        cp.start()
        stage3.append(cp)

    load_top.wait()
    k, n = iota((512, 512), 0), iota((512, 512), 1)
    target = (((k >> 4) & 3) << 7) + ((k >> 7) << 5) + (((k >> 6) & 1) << 4) + (k & 15)
    perm[...] = jnp.where(n == target, 1.0, 0.0).astype(BF16)

    def reorder(g, carry):
        parts = []
        for half in range(2):
            pieces = [
                kv[:, pl.ds(pl.multiple_of(((half * 4 + z4) * 16 + g) * 128, 128), 128)] for z4 in range(4)
            ]
            parts.append(jnp.concatenate(pieces, axis=1))
        got = nn(jnp.concatenate(parts, axis=0), perm[...]).astype(BF16)
        for half in range(2):
            for x in range(4):
                kp[x, g, :, pl.ds(half * 128, 128)] = got[half * 64 : half * 64 + 64, x * 128 : x * 128 + 128]
        return carry

    lax.fori_loop(0, NGY, reorder, 0)

    r, c = iota((32, 384), 0), iota((32, 384), 1)
    t, e, right = (r >> 2) & 3, r & 3, r >= 16
    spot = jnp.where(
        t < 2, t * 128 + jnp.where(right, 124, 0), 256 + (t & 1) * 64 + jnp.where(right, 60, 0)
    )
    pick = jnp.where(c == spot + e, 1.0, 0.0).astype(BF16)

    def zy_pass(p, carry):
        pair = jnp.concatenate([fld[2 * p], fld[2 * p + 1]], axis=1)
        near = jnp.concatenate([halo[2 * p], halo[2 * p + 1]], axis=1)
        got = (
            nn(wf[0, :, pl.ds(0, 256)], pair) + nn(wf[0, :, pl.ds(256, 320)], near)
            + nn(wf[1, :, pl.ds(0, 256)], pair) + nn(wf[1, :, pl.ds(256, 320)], near)
        )
        cells = jnp.concatenate([cl[p].reshape(64, 128), ch[p].reshape(192, 128)], axis=0)
        got_coarse = nn(wc[0], cells) + nn(wc[1], cells)
        both = jnp.concatenate([got.astype(BF16), got_coarse.astype(BF16)], axis=1)
        tt[p] = both
        ends = nt(pick, both).astype(BF16)
        edge_out[0, p] = ends[:16]
        edge_out[1, p] = ends[16:]
        return carry

    edges = []
    for cp in coarse:
        cp.wait()
    for h in range(NCH):
        for cp in fine[h]:
            cp.wait()
        lax.fori_loop(h * PCH, (h + 1) * PCH, zy_pass, 0)
        ps = pl.ds(h * PCH, PCH)
        left = remote(edge_out.at[0, ps], edge_in.at[1, ps], es.at[h, 0], er.at[h, 0], dev(-1, 0, 0))
        right = remote(edge_out.at[1, ps], edge_in.at[0, ps], es.at[h, 1], er.at[h, 1], dev(1, 0, 0))
        left.start()
        right.start()
        edges.append((left, right))

    def x_pass(p, carry):
        both = tt[p]
        ends = jnp.concatenate([edge_in[0, p], edge_in[1, p]], axis=0)
        base[p] = nn(both, xw[0]) + nn(both, xw[1]) + tn(jnp.concatenate([ends, ends], axis=0), xh[...])
        return carry

    for h in range(NCH):
        for cp in edges[h]:
            cp.wait()
        lax.fori_loop(h * PCH, (h + 1) * PCH, x_pass, 0)

    def gather_dot(x):
        def add(g, total):
            block = jnp.concatenate([gath[x, g, 0], gath[x, g, 1]], axis=1)
            return total + nt(kp[x, g], block)

        acc[...] = acc[...] + lax.fori_loop(0, NGY, add, jnp.zeros((64, 16), F32))

    acc[...] = jnp.zeros((64, 16), F32)
    gather_dot(gx)
    for d in range(1, NGX):
        stage3[d - 1].wait()
        gather_dot(lax.rem(gx + (NGX - d), NGX))

    k, n = iota((64, 512), 0), iota((64, 512), 1)
    spread = jnp.where(k == ((n >> 7) << 4) + ((n & 127) >> 3), 1.0, 0.0).astype(BF16)
    sums = acc[...]
    hi, lo = hi_lo(sums)
    lo2 = (sums - hi.astype(F32) - lo.astype(F32)).astype(BF16)
    prol[...] = tn(hi, spread) + tn(lo, spread) + tn(lo2, spread)

    for p in range(8):
        for v in range(2):
            for zt in range(2):
                for yt in range(2):
                    row = prol[pl.ds(2 * p + v, 1), pl.ds((zt * 2 + yt) * 128, 128)]
                    block = jnp.broadcast_to(row, (8, 128))
                    for i in range(8):
                        rows = pl.ds((zt * 8 + i) * 16 + yt * 8, 8)
                        base[p, rows, pl.ds(v * 128, 128)] = base[p, rows, pl.ds(v * 128, 128)] + block

    def finish(p, carry):
        for v in range(2):
            res[2 * p + v] = base[p, :, pl.ds(v * 128, 128)].astype(BF16)
        return carry

    lax.fori_loop(0, 8, finish, 0)
    store = pltpu.make_async_copy(res, out, osem.at[0])
    store.start()
    store.wait()


def shards(field, fine_taps, coarse_taps, top_kernel):
    vm = pltpu.VMEM
    dma = pltpu.SemaphoreType.DMA
    hbm = pl.BlockSpec(memory_space=pltpu.HBM)
    out = pl.pallas_call(
        kernel,
        name="covariance",
        out_shape=jax.ShapeDtypeStruct((16, 256, 128), BF16),
        in_specs=[hbm, hbm, hbm, hbm],
        out_specs=hbm,
        scratch_shapes=[
            pltpu.SMEM((3, 9), F32),
            pltpu.SMEM((3, 9), F32),
            vm((16, 256, 128), BF16),
            vm((16, 320, 128), BF16),
            vm((2, 16, 64, 128), BF16),
            vm((8, 2, 2, 16, 128), BF16),
            vm((8, 12, 16, 128), BF16),
            vm((8, 256, 384), BF16),
            vm((2, 8, 16, 256), BF16),
            vm((2, 8, 16, 256), BF16),
            vm((8, 256, 256), F32),
            vm((16, 256, 128), BF16),
            vm((2, 256, 576), BF16),
            vm((2, 256, 256), BF16),
            vm((2, 384, 256), BF16),
            vm((64, 256), BF16),
            vm((192, 256), BF16),
            vm((512, 128), BF16),
            vm((512, 512), BF16),
            vm((64, 16384), BF16),
            vm((4, 16, 64, 256), BF16),
            vm((4, 16, 2, 16, 128), BF16),
            vm((4, 16, 128), BF16),
            vm((16, 512), F32),
            vm((64, 16), F32),
            vm((16, 512), F32),
            dma((NCH, 8)), dma((NCH, 8)),
            dma((8,)), dma((8,)),
            dma((NCH, 2)), dma((NCH, 2)),
            dma((3,)), dma((3,)),
            dma((15,)), dma((15,)),
            dma((3,)), dma((3,)),
            dma((4,)), dma((1,)),
        ],
        compiler_params=pltpu.CompilerParams(
            collective_id=1, has_side_effects=True, vmem_limit_bytes=60 << 20
        ),
    )(field.reshape(16, 256, 128), fine_taps, coarse_taps, top_kernel.reshape(64, 16384))
    return out.reshape(field.shape)


def solution(mesh):
    return jax.shard_map(
        shards,
        mesh=mesh,
        in_specs=(P(None, "gz", "gy", "gx"), P(), P(), P("gz", "gy", "gx", None)),
        out_specs=P(None, "gz", "gy", "gx"),
        check_vma=False,
    )
```

```python
import functools

import jax
import jax.numpy as jnp
from jax import lax
from jax.experimental import pallas as pl
from jax.experimental.pallas import tpu as pltpu
from jax.sharding import PartitionSpec as P

F32 = jnp.float32
BF16 = jnp.bfloat16
MESH = pl.DeviceIdType.MESH
NGX, NGY, NGZ = 4, 16, 4
NCH = 2
VCH = 16 // NCH
PCH = 8 // NCH
SIDES = [(1, 0), (-1, 0), (0, 1), (0, -1), (1, 1), (1, -1), (-1, 1), (-1, -1)]


def iota(shape, dim):
    return lax.broadcasted_iota(jnp.int32, shape, dim)


def nn(a, b):
    return lax.dot_general(a, b, (((1,), (0,)), ((), ())), preferred_element_type=F32)


def nt(a, b):
    return lax.dot_general(a, b, (((1,), (1,)), ((), ())), preferred_element_type=F32)


def tn(a, b):
    return lax.dot_general(a, b, (((0,), (0,)), ((), ())), preferred_element_type=F32)


def hi_lo(w):
    hi = w.astype(BF16)
    return hi, (w - hi.astype(F32)).astype(BF16)


def taps_at(taps_ref, row, offset):
    value = jnp.zeros(offset.shape, F32)
    for k in range(9):
        value = jnp.where(offset == k, taps_ref[row, k], value)
    return value


def kernel(
    field, fine_hbm, coarse_hbm, top, out,
    fine_taps, coarse_taps,
    fld, halo, strips, cl, ch, tt, edge_out, edge_in, base, res,
    wf, wc, xw, xh, gsel, rx, perm, kv, kp, gath, tile_in, psum, prol,
    fs, fr, cs, cr, es, er, s1s, s1r, s2s, s2r, s3s, s3r, lsem, osem,
):
    gx, gy, gz = lax.axis_index("gx"), lax.axis_index("gy"), lax.axis_index("gz")

    def dev(dx, dy, dz):
        return (
            lax.rem(gx + (dx + NGX), NGX),
            lax.rem(gy + (dy + NGY), NGY),
            lax.rem(gz + (dz + NGZ), NGZ),
        )

    def remote(src, dst, ssem, rsem, to):
        return pltpu.make_async_remote_copy(
            src_ref=src, dst_ref=dst, send_sem=ssem, recv_sem=rsem, device_id=to, device_id_type=MESH
        )

    load_field = pltpu.make_async_copy(field, fld, lsem.at[0])
    load_top = pltpu.make_async_copy(top, kv, lsem.at[1])
    load_fine = pltpu.make_async_copy(fine_hbm, fine_taps, lsem.at[2])
    load_coarse = pltpu.make_async_copy(coarse_hbm, coarse_taps, lsem.at[3])
    load_field.start()
    load_fine.start()
    load_coarse.start()
    load_top.start()

    barrier = pltpu.get_barrier_semaphore()
    partners = [(i, 0, 0) for i in range(1, NGX)] + [(0, i, 0) for i in range(1, NGY)]
    partners += [(0, 0, i) for i in range(1, NGZ)] + [(0, dy, dz) for dz, dy in SIDES[4:]]
    for d in partners:
        pl.semaphore_signal(barrier, inc=1, device_id=dev(*d), device_id_type=MESH)

    r, c = iota((192, 256), 0), iota((192, 256), 1)
    z, y = c >> 4, c & 15
    strip_z, strip_y = (r & 63) >> 2, (r & 3) + jnp.where(r >= 64, 12, 0)
    q = r - 128
    cz, cy = ((q >> 5) << 2) + ((q >> 2) & 3), (((q >> 4) & 1) << 2) + (q & 3)
    is_strip = (z == strip_z) & (y == strip_y)
    is_mean = ((z >> 1) == cz) & ((y >> 1) == cy)
    gsel[...] = jnp.where(
        r < 128, jnp.where(is_strip, 1.0, 0.0), jnp.where(is_mean, 0.25, 0.0)
    ).astype(BF16)
    k, n = iota((512, 128), 0), iota((512, 128), 1)
    rx[...] = jnp.where(((k >> 8) == (n >> 6)) & (((k & 127) >> 1) == (n & 63)), 0.5, 0.0).astype(BF16)

    load_field.wait()
    r, c = iota((32, 256), 0), iota((32, 256), 1)
    rows = jnp.where(((r & 15) == (c >> 4)) & (((c & 15) >> 3) == (r >> 4)), 1.0, 0.0).astype(BF16)
    for zt in range(2):
        total = fld[:, pl.ds(zt * 128, 16), :].astype(F32)
        for i in range(1, 8):
            total = total + fld[:, pl.ds(zt * 128 + i * 16, 16), :].astype(F32)
        total = total.reshape(256, 128)
        hi, lo = hi_lo(total)
        lo2 = (total - hi.astype(F32) - lo.astype(F32)).astype(BF16)
        both = nn(rows, hi) + nn(rows, lo) + nn(rows, lo2)
        for yt in range(2):
            psum[:, pl.ds((zt * 2 + yt) * 128, 128)] = both[yt * 16 : yt * 16 + 16]
    k, n = iota((512, 128), 0), iota((512, 128), 1)
    spot = lax.rem(gz, 2) * 64 + ((k >> 7) << 4) + ((k & 127) >> 3)
    place = jnp.where(n == spot, 1.0 / 512.0, 0.0).astype(BF16)
    sums = psum[...]
    hi, lo = hi_lo(sums)
    lo2 = (sums - hi.astype(F32) - lo.astype(F32)).astype(BF16)
    tile_in[gz] = (nn(hi, place) + nn(lo, place) + nn(lo2, place)).astype(BF16)

    pl.semaphore_wait(barrier, len(partners))

    stage1 = []
    for d in range(1, NGZ):
        cp = remote(tile_in.at[gz], tile_in.at[gz], s1s.at[d - 1], s1r.at[d - 1], dev(0, 0, d))
        cp.start()
        stage1.append(cp)

    def fine_copy(h, i):
        dz, dy = SIDES[i]
        vs = pl.ds(h * VCH, VCH)
        if dy == 0:
            src = fld.at[vs, pl.ds(192 if dz > 0 else 0, 64)]
            dst = halo.at[vs, pl.ds(0 if dz > 0 else 64, 64)]
        elif dz == 0:
            src = strips.at[1 if dy > 0 else 0, vs]
            dst = halo.at[vs, pl.ds(128 if dy > 0 else 192, 64)]
        else:
            src = strips.at[1 if dy > 0 else 0, vs, pl.ds(48 if dz > 0 else 0, 16)]
            dst = halo.at[vs, pl.ds(256 + (0 if dz > 0 else 32) + (0 if dy > 0 else 16), 16)]
        return remote(src, dst, fs.at[h, i], fr.at[h, i], dev(0, dy, dz))

    def coarse_copy(i):
        dz, dy = SIDES[i]
        if dy == 0:
            src, dst = cl.at[:, 1 if dz > 0 else 0], ch.at[:, pl.ds(0 if dz > 0 else 2, 2)]
        elif dz == 0:
            src, dst = cl.at[:, :, 1 if dy > 0 else 0], ch.at[:, pl.ds(4 if dy > 0 else 6, 2)]
        else:
            src = cl.at[:, 1 if dz > 0 else 0, 1 if dy > 0 else 0]
            dst = ch.at[:, 8 + (0 if dz > 0 else 2) + (0 if dy > 0 else 1)]
        return remote(src, dst, cs.at[i], cr.at[i], dev(0, dy, dz))

    fine = [[fine_copy(h, i) for i in range(8)] for h in range(NCH)]
    coarse = [coarse_copy(i) for i in range(8)]
    for h in range(NCH):
        fine[h][0].start()
        fine[h][1].start()

    def cut(p, carry):
        pair = jnp.concatenate([fld[2 * p], fld[2 * p + 1]], axis=1)
        got = nn(gsel[...], pair)
        for v in range(2):
            for side in range(2):
                strips[side, 2 * p + v] = got[side * 64 : side * 64 + 64, v * 128 : v * 128 + 128].astype(BF16)
        means = got[128:192]
        hi, lo = hi_lo(means)
        both = jnp.concatenate([hi[:, :128], lo[:, :128], hi[:, 128:], lo[:, 128:]], axis=1)
        cl[p] = nn(both, rx[...]).astype(BF16).reshape(2, 2, 16, 128)
        return carry

    lax.fori_loop(0, 8, cut, 0, unroll=4)
    for i in range(2, 8):
        fine[0][i].start()
    for i in range(8):
        coarse[i].start()
    for h in range(1, NCH):
        for i in range(2, 8):
            fine[h][i].start()

    for cp in stage1:
        cp.wait()
    for half in range(2):
        gath[gx, gy, half] = tile_in[2 * half] + tile_in[2 * half + 1]
    stage2 = []
    for d in range(1, NGY):
        cp = remote(gath.at[gx, gy], gath.at[gx, gy], s2s.at[d - 1], s2r.at[d - 1], dev(0, d, 0))
        cp.start()
        stage2.append(cp)

    load_fine.wait()
    load_coarse.wait()
    zmin, zmax = jnp.where(gz > 0, -99, 0), jnp.where(gz < NGZ - 1, 99, 0)
    ymin, ymax = jnp.where(gy > 0, -99, 0), jnp.where(gy < NGY - 1, 99, 0)

    def zy_weights(taps_ref, zi, yi, zo, yo, side):
        ok = (zi >= zmin) & (yi >= ymin) & (zi < zmax + side) & (yi < ymax + side)
        w = taps_at(taps_ref, 0, zi - zo + 4) * taps_at(taps_ref, 1, yi - yo + 4)
        return hi_lo(jnp.where(ok, w, 0.0))

    o, c = iota((256, 256), 0), iota((256, 256), 1)
    hi, lo = zy_weights(fine_taps, c >> 4, c & 15, o >> 4, o & 15, 16)
    wf[0, :, pl.ds(0, 256)] = hi
    wf[1, :, pl.ds(0, 256)] = lo
    o, c = iota((256, 320), 0), iota((256, 320), 1)
    z4, y4, q = (c >> 2) & 3, c & 3, (c >> 4) & 3
    zi = jnp.where(
        c < 64, (c >> 4) - 4, jnp.where(c < 128, (c >> 4) + 12, jnp.where(c < 256, (c & 63) >> 2, jnp.where(q < 2, z4 - 4, z4 + 16)))
    )
    yi = jnp.where(
        c < 128, c & 15, jnp.where(c < 192, y4 - 4, jnp.where(c < 256, y4 + 16, jnp.where((q & 1) == 0, y4 - 4, y4 + 16)))
    )
    hi, lo = zy_weights(fine_taps, zi, yi, o >> 4, o & 15, 16)
    wf[0, :, pl.ds(256, 320)] = hi
    wf[1, :, pl.ds(256, 320)] = lo
    o, c = iota((256, 256), 0), iota((256, 256), 1)
    z4, y4, q = (c >> 2) & 3, c & 3, c >> 4
    first = (q & 1) * 4
    zi = jnp.where(
        q < 4, ((q >> 1) << 2) + z4,
        jnp.where(q < 6, z4 - 4, jnp.where(q < 8, z4 + 8, jnp.where(q < 12, first + z4, jnp.where(q < 14, z4 - 4, z4 + 8)))),
    )
    yi = jnp.where(
        q < 8, first + y4,
        jnp.where(q < 10, y4 - 4, jnp.where(q < 12, y4 + 8, jnp.where((q & 1) == 0, y4 - 4, y4 + 8))),
    )
    hi, lo = zy_weights(coarse_taps, zi, yi, o >> 5, (o & 15) >> 1, 8)
    wc[0] = hi
    wc[1] = lo

    k, n = iota((384, 256), 0), iota((384, 256), 1)
    xo, v = n & 127, n >> 7
    w = jnp.where(
        k < 256,
        jnp.where((k >> 7) == v, taps_at(fine_taps, 2, (k & 127) - xo + 4), 0.0),
        jnp.where(((k >> 6) & 1) == v, taps_at(coarse_taps, 2, (k & 63) - (xo >> 1) + 4), 0.0),
    )
    hi, lo = hi_lo(w)
    xw[0] = hi
    xw[1] = lo
    r, n = iota((32, 256), 0), iota((32, 256), 1)
    xo, v, e = n & 127, n >> 7, r & 3
    right = r >= 16
    w = jnp.where(
        (r & 8) == 0,
        taps_at(fine_taps, 2, e + jnp.where(right, 128, -4) - xo + 4),
        taps_at(coarse_taps, 2, e + jnp.where(right, 64, -4) - (xo >> 1) + 4),
    )
    there = jnp.where(right, jnp.where(gx < NGX - 1, 1, 0), jnp.where(gx > 0, 1, 0)) == 1
    hi, lo = hi_lo(jnp.where(there & (((r >> 2) & 1) == v), w, 0.0))
    xh[pl.ds(0, 32)] = hi
    xh[pl.ds(32, 32)] = lo

    for cp in stage2:
        cp.wait()
    stage3 = []
    for d in range(1, NGX):
        cp = remote(gath.at[gx], gath.at[gx], s3s.at[d - 1], s3r.at[d - 1], dev(d, 0, 0))
        cp.start()
        stage3.append(cp)

    load_top.wait()
    k, n = iota((512, 512), 0), iota((512, 512), 1)
    target = (((k >> 4) & 3) << 7) + ((k >> 7) << 5) + (((k >> 6) & 1) << 4) + (k & 15)
    perm[...] = jnp.where(n == target, 1.0, 0.0).astype(BF16)

    def reorder(i, carry):
        parts = []
        for g in range(4):
            for half in range(2):
                pieces = [
                    kv[:, pl.ds(pl.multiple_of(((half * 4 + z4) * 16 + i * 4 + g) * 128, 128), 128)]
                    for z4 in range(4)
                ]
                parts.append(jnp.concatenate(pieces, axis=1))
        got = nn(jnp.concatenate(parts, axis=0), perm[...]).astype(BF16)
        for g in range(8):
            at = pl.ds(pl.multiple_of((i * 8 + g) * 128, 128), 128)
            for x in range(4):
                kp[x, :, at] = got[g * 64 : g * 64 + 64, x * 128 : x * 128 + 128]
        return carry

    lax.fori_loop(0, 4, reorder, 0)

    r, c = iota((32, 384), 0), iota((32, 384), 1)
    t, e, right = (r >> 2) & 3, r & 3, r >= 16
    spot = jnp.where(
        t < 2, t * 128 + jnp.where(right, 124, 0), 256 + (t & 1) * 64 + jnp.where(right, 60, 0)
    )
    pick = jnp.where(c == spot + e, 1.0, 0.0).astype(BF16)

    def zy_pass(p, carry):
        pair = jnp.concatenate([fld[2 * p], fld[2 * p + 1]], axis=1)
        near = jnp.concatenate([halo[2 * p], halo[2 * p + 1]], axis=1)
        got = (
            nn(wf[0, :, pl.ds(0, 256)], pair) + nn(wf[0, :, pl.ds(256, 320)], near)
            + nn(wf[1, :, pl.ds(0, 256)], pair) + nn(wf[1, :, pl.ds(256, 320)], near)
        )
        cells = jnp.concatenate([cl[p].reshape(64, 128), ch[p].reshape(192, 128)], axis=0)
        got_coarse = nn(wc[0], cells) + nn(wc[1], cells)
        both = jnp.concatenate([got.astype(BF16), got_coarse.astype(BF16)], axis=1)
        tt[p] = both
        ends = nt(pick, both).astype(BF16)
        edge_out[0, p] = ends[:16]
        edge_out[1, p] = ends[16:]
        return carry

    edges = []
    for cp in coarse:
        cp.wait()
    for h in range(NCH):
        for cp in fine[h]:
            cp.wait()
        lax.fori_loop(h * PCH, (h + 1) * PCH, zy_pass, 0, unroll=2)
        ps = pl.ds(h * PCH, PCH)
        left = remote(edge_out.at[0, ps], edge_in.at[1, ps], es.at[h, 0], er.at[h, 0], dev(-1, 0, 0))
        right = remote(edge_out.at[1, ps], edge_in.at[0, ps], es.at[h, 1], er.at[h, 1], dev(1, 0, 0))
        left.start()
        right.start()
        edges.append((left, right))

    def x_pass(p, carry):
        both = tt[p]
        ends = jnp.concatenate([edge_in[0, p], edge_in[1, p]], axis=0)
        base[p] = nn(both, xw[0]) + nn(both, xw[1]) + tn(jnp.concatenate([ends, ends], axis=0), xh[...])
        return carry

    for h in range(NCH):
        for cp in edges[h]:
            cp.wait()
        lax.fori_loop(h * PCH, (h + 1) * PCH, x_pass, 0, unroll=2)

    def gather_dot(x):
        tiles = [gath[x, g, half] for g in range(NGY) for half in range(2)]
        return nt(kp[x], jnp.concatenate(tiles, axis=1))

    sums = gather_dot(gx)
    for d in range(1, NGX):
        stage3[d - 1].wait()
        sums = sums + gather_dot(lax.rem(gx + (NGX - d), NGX))

    k, n = iota((64, 512), 0), iota((64, 512), 1)
    spread = jnp.where(k == ((n >> 7) << 4) + ((n & 127) >> 3), 1.0, 0.0).astype(BF16)
    hi, lo = hi_lo(sums)
    lo2 = (sums - hi.astype(F32) - lo.astype(F32)).astype(BF16)
    prol[...] = tn(hi, spread) + tn(lo, spread) + tn(lo2, spread)

    def finish(p, carry):
        for v in range(2):
            for zt in range(2):
                rows = [
                    prol[pl.ds(2 * p + v, 1), pl.ds((zt * 2 + yt) * 128, 128)] for yt in range(2)
                ]
                block = jnp.concatenate([jnp.broadcast_to(row, (8, 128)) for row in rows], axis=0)
                for i in range(8):
                    at = pl.ds((zt * 8 + i) * 16, 16)
                    res[2 * p + v, at] = (base[p, at, pl.ds(v * 128, 128)] + block).astype(BF16)
        return carry

    stores = []
    for h in range(4):
        lax.fori_loop(h * 2, h * 2 + 2, finish, 0, unroll=True)
        vs = pl.ds(h * 4, 4)
        stores.append(pltpu.make_async_copy(res.at[vs], out.at[vs], osem.at[h]))
        stores[h].start()
    for cp in stores:
        cp.wait()


def shards(field, fine_taps, coarse_taps, top_kernel):
    vm = pltpu.VMEM
    dma = pltpu.SemaphoreType.DMA
    hbm = pl.BlockSpec(memory_space=pltpu.HBM)
    out = pl.pallas_call(
        kernel,
        name="covariance",
        out_shape=jax.ShapeDtypeStruct((16, 256, 128), BF16),
        in_specs=[hbm, hbm, hbm, hbm],
        out_specs=hbm,
        scratch_shapes=[
            pltpu.SMEM((3, 9), F32),
            pltpu.SMEM((3, 9), F32),
            vm((16, 256, 128), BF16),
            vm((16, 320, 128), BF16),
            vm((2, 16, 64, 128), BF16),
            vm((8, 2, 2, 16, 128), BF16),
            vm((8, 12, 16, 128), BF16),
            vm((8, 256, 384), BF16),
            vm((2, 8, 16, 256), BF16),
            vm((2, 8, 16, 256), BF16),
            vm((8, 256, 256), F32),
            vm((16, 256, 128), BF16),
            vm((2, 256, 576), BF16),
            vm((2, 256, 256), BF16),
            vm((2, 384, 256), BF16),
            vm((64, 256), BF16),
            vm((192, 256), BF16),
            vm((512, 128), BF16),
            vm((512, 512), BF16),
            vm((64, 16384), BF16),
            vm((4, 64, 4096), BF16),
            vm((4, 16, 2, 16, 128), BF16),
            vm((4, 16, 128), BF16),
            vm((16, 512), F32),
            vm((16, 512), F32),
            dma((NCH, 8)), dma((NCH, 8)),
            dma((8,)), dma((8,)),
            dma((NCH, 2)), dma((NCH, 2)),
            dma((3,)), dma((3,)),
            dma((15,)), dma((15,)),
            dma((3,)), dma((3,)),
            dma((4,)), dma((4,)),
        ],
        compiler_params=pltpu.CompilerParams(
            collective_id=1, has_side_effects=True, vmem_limit_bytes=60 << 20
        ),
    )(field.reshape(16, 256, 128), fine_taps, coarse_taps, top_kernel.reshape(64, 16384))
    return out.reshape(field.shape)


def solution(mesh):
    return jax.shard_map(
        shards,
        mesh=mesh,
        in_specs=(P(None, "gz", "gy", "gx"), P(), P(), P("gz", "gy", "gx", None)),
        out_specs=P(None, "gz", "gy", "gx"),
        check_vma=False,
    )
```

```python
import functools

import jax
import jax.numpy as jnp
from jax import lax
from jax.experimental import pallas as pl
from jax.experimental.pallas import tpu as pltpu
from jax.sharding import PartitionSpec as P

F32 = jnp.float32
BF16 = jnp.bfloat16
MESH = pl.DeviceIdType.MESH
NGX, NGY, NGZ = 4, 16, 4
NCH = 2
VCH = 16 // NCH
PCH = 8 // NCH
SIDES = [(1, 0), (-1, 0), (0, 1), (0, -1), (1, 1), (1, -1), (-1, 1), (-1, -1)]


def iota(shape, dim):
    return lax.broadcasted_iota(jnp.int32, shape, dim)


def nn(a, b):
    return lax.dot_general(a, b, (((1,), (0,)), ((), ())), preferred_element_type=F32)


def nt(a, b):
    return lax.dot_general(a, b, (((1,), (1,)), ((), ())), preferred_element_type=F32)


def tn(a, b):
    return lax.dot_general(a, b, (((0,), (0,)), ((), ())), preferred_element_type=F32)


def hi_lo(w):
    hi = w.astype(BF16)
    return hi, (w - hi.astype(F32)).astype(BF16)


def taps_at(taps_ref, row, offset):
    value = jnp.zeros(offset.shape, F32)
    for k in range(9):
        value = jnp.where(offset == k, taps_ref[row, k], value)
    return value


def kernel(
    field, fine_hbm, coarse_hbm, top, out,
    fine_taps, coarse_taps,
    fld, halo, strips, cl, ch, tt, edge_out, edge_in, base,
    wf, wc, xw, xh, gsel, rx, perm, kv, kp, gath, tile_in, psum, prol,
    fs, fr, cs, cr, es, er, s1s, s1r, s2s, s2r, s3s, s3r, lsem,
):
    gx, gy, gz = lax.axis_index("gx"), lax.axis_index("gy"), lax.axis_index("gz")

    def dev(dx, dy, dz):
        return (
            lax.rem(gx + (dx + NGX), NGX),
            lax.rem(gy + (dy + NGY), NGY),
            lax.rem(gz + (dz + NGZ), NGZ),
        )

    def remote(src, dst, ssem, rsem, to):
        return pltpu.make_async_remote_copy(
            src_ref=src, dst_ref=dst, send_sem=ssem, recv_sem=rsem, device_id=to, device_id_type=MESH
        )

    load_field = pltpu.make_async_copy(field, fld, lsem.at[0])
    load_top = pltpu.make_async_copy(top, kv, lsem.at[1])
    load_fine = pltpu.make_async_copy(fine_hbm, fine_taps, lsem.at[2])
    load_coarse = pltpu.make_async_copy(coarse_hbm, coarse_taps, lsem.at[3])
    load_field.start()
    load_fine.start()
    load_coarse.start()
    load_top.start()

    barrier = pltpu.get_barrier_semaphore()
    partners = [(i, 0, 0) for i in range(1, NGX)] + [(0, i, 0) for i in range(1, NGY)]
    partners += [(0, 0, i) for i in range(1, NGZ)] + [(0, dy, dz) for dz, dy in SIDES[4:]]
    for d in partners:
        pl.semaphore_signal(barrier, inc=1, device_id=dev(*d), device_id_type=MESH)

    r, c = iota((192, 256), 0), iota((192, 256), 1)
    z, y = c >> 4, c & 15
    strip_z, strip_y = (r & 63) >> 2, (r & 3) + jnp.where(r >= 64, 12, 0)
    q = r - 128
    cz, cy = ((q >> 5) << 2) + ((q >> 2) & 3), (((q >> 4) & 1) << 2) + (q & 3)
    is_strip = (z == strip_z) & (y == strip_y)
    is_mean = ((z >> 1) == cz) & ((y >> 1) == cy)
    gsel[...] = jnp.where(
        r < 128, jnp.where(is_strip, 1.0, 0.0), jnp.where(is_mean, 0.25, 0.0)
    ).astype(BF16)
    k, n = iota((512, 128), 0), iota((512, 128), 1)
    rx[...] = jnp.where(((k >> 8) == (n >> 6)) & (((k & 127) >> 1) == (n & 63)), 0.5, 0.0).astype(BF16)

    load_field.wait()
    r, c = iota((32, 256), 0), iota((32, 256), 1)
    rows = jnp.where(((r & 15) == (c >> 4)) & (((c & 15) >> 3) == (r >> 4)), 1.0, 0.0).astype(BF16)
    for zt in range(2):
        total = fld[:, pl.ds(zt * 128, 16), :].astype(F32)
        for i in range(1, 8):
            total = total + fld[:, pl.ds(zt * 128 + i * 16, 16), :].astype(F32)
        total = total.reshape(256, 128)
        hi, lo = hi_lo(total)
        lo2 = (total - hi.astype(F32) - lo.astype(F32)).astype(BF16)
        both = nn(rows, hi) + nn(rows, lo) + nn(rows, lo2)
        for yt in range(2):
            psum[:, pl.ds((zt * 2 + yt) * 128, 128)] = both[yt * 16 : yt * 16 + 16]
    k, n = iota((512, 128), 0), iota((512, 128), 1)
    spot = lax.rem(gz, 2) * 64 + ((k >> 7) << 4) + ((k & 127) >> 3)
    place = jnp.where(n == spot, 1.0 / 512.0, 0.0).astype(BF16)
    sums = psum[...]
    hi, lo = hi_lo(sums)
    lo2 = (sums - hi.astype(F32) - lo.astype(F32)).astype(BF16)
    tile_in[gz] = (nn(hi, place) + nn(lo, place) + nn(lo2, place)).astype(BF16)

    pl.semaphore_wait(barrier, len(partners))

    stage1 = []
    for d in range(1, NGZ):
        cp = remote(tile_in.at[gz], tile_in.at[gz], s1s.at[d - 1], s1r.at[d - 1], dev(0, 0, d))
        cp.start()
        stage1.append(cp)

    def fine_copy(h, i):
        dz, dy = SIDES[i]
        vs = pl.ds(h * VCH, VCH)
        if dy == 0:
            src = fld.at[vs, pl.ds(192 if dz > 0 else 0, 64)]
            dst = halo.at[vs, pl.ds(0 if dz > 0 else 64, 64)]
        elif dz == 0:
            src = strips.at[1 if dy > 0 else 0, vs]
            dst = halo.at[vs, pl.ds(128 if dy > 0 else 192, 64)]
        else:
            src = strips.at[1 if dy > 0 else 0, vs, pl.ds(48 if dz > 0 else 0, 16)]
            dst = halo.at[vs, pl.ds(256 + (0 if dz > 0 else 32) + (0 if dy > 0 else 16), 16)]
        return remote(src, dst, fs.at[h, i], fr.at[h, i], dev(0, dy, dz))

    def coarse_copy(i):
        dz, dy = SIDES[i]
        if dy == 0:
            src, dst = cl.at[:, 1 if dz > 0 else 0], ch.at[:, pl.ds(0 if dz > 0 else 2, 2)]
        elif dz == 0:
            src, dst = cl.at[:, :, 1 if dy > 0 else 0], ch.at[:, pl.ds(4 if dy > 0 else 6, 2)]
        else:
            src = cl.at[:, 1 if dz > 0 else 0, 1 if dy > 0 else 0]
            dst = ch.at[:, 8 + (0 if dz > 0 else 2) + (0 if dy > 0 else 1)]
        return remote(src, dst, cs.at[i], cr.at[i], dev(0, dy, dz))

    fine = [[fine_copy(h, i) for i in range(8)] for h in range(NCH)]
    coarse = [coarse_copy(i) for i in range(8)]
    for h in range(NCH):
        fine[h][0].start()
        fine[h][1].start()

    def cut(p, carry):
        pair = jnp.concatenate([fld[2 * p], fld[2 * p + 1]], axis=1)
        got = nn(gsel[...], pair)
        for v in range(2):
            for side in range(2):
                strips[side, 2 * p + v] = got[side * 64 : side * 64 + 64, v * 128 : v * 128 + 128].astype(BF16)
        means = got[128:192]
        hi, lo = hi_lo(means)
        both = jnp.concatenate([hi[:, :128], lo[:, :128], hi[:, 128:], lo[:, 128:]], axis=1)
        cl[p] = nn(both, rx[...]).astype(BF16).reshape(2, 2, 16, 128)
        return carry

    lax.fori_loop(0, 8, cut, 0, unroll=4)
    for i in range(2, 8):
        fine[0][i].start()
    for i in range(8):
        coarse[i].start()
    for h in range(1, NCH):
        for i in range(2, 8):
            fine[h][i].start()

    for cp in stage1:
        cp.wait()
    for half in range(2):
        gath[gx, gy, half] = tile_in[2 * half] + tile_in[2 * half + 1]
    stage2 = []
    for d in range(1, NGY):
        cp = remote(gath.at[gx, gy], gath.at[gx, gy], s2s.at[d - 1], s2r.at[d - 1], dev(0, d, 0))
        cp.start()
        stage2.append(cp)

    load_fine.wait()
    load_coarse.wait()
    zmin, zmax = jnp.where(gz > 0, -99, 0), jnp.where(gz < NGZ - 1, 99, 0)
    ymin, ymax = jnp.where(gy > 0, -99, 0), jnp.where(gy < NGY - 1, 99, 0)

    def zy_weights(taps_ref, zi, yi, zo, yo, side):
        ok = (zi >= zmin) & (yi >= ymin) & (zi < zmax + side) & (yi < ymax + side)
        w = taps_at(taps_ref, 0, zi - zo + 4) * taps_at(taps_ref, 1, yi - yo + 4)
        return hi_lo(jnp.where(ok, w, 0.0))

    o, c = iota((256, 256), 0), iota((256, 256), 1)
    hi, lo = zy_weights(fine_taps, c >> 4, c & 15, o >> 4, o & 15, 16)
    wf[0, :, pl.ds(0, 256)] = hi
    wf[1, :, pl.ds(0, 256)] = lo
    o, c = iota((256, 320), 0), iota((256, 320), 1)
    z4, y4, q = (c >> 2) & 3, c & 3, (c >> 4) & 3
    zi = jnp.where(
        c < 64, (c >> 4) - 4, jnp.where(c < 128, (c >> 4) + 12, jnp.where(c < 256, (c & 63) >> 2, jnp.where(q < 2, z4 - 4, z4 + 16)))
    )
    yi = jnp.where(
        c < 128, c & 15, jnp.where(c < 192, y4 - 4, jnp.where(c < 256, y4 + 16, jnp.where((q & 1) == 0, y4 - 4, y4 + 16)))
    )
    hi, lo = zy_weights(fine_taps, zi, yi, o >> 4, o & 15, 16)
    wf[0, :, pl.ds(256, 320)] = hi
    wf[1, :, pl.ds(256, 320)] = lo
    o, c = iota((256, 256), 0), iota((256, 256), 1)
    z4, y4, q = (c >> 2) & 3, c & 3, c >> 4
    first = (q & 1) * 4
    zi = jnp.where(
        q < 4, ((q >> 1) << 2) + z4,
        jnp.where(q < 6, z4 - 4, jnp.where(q < 8, z4 + 8, jnp.where(q < 12, first + z4, jnp.where(q < 14, z4 - 4, z4 + 8)))),
    )
    yi = jnp.where(
        q < 8, first + y4,
        jnp.where(q < 10, y4 - 4, jnp.where(q < 12, y4 + 8, jnp.where((q & 1) == 0, y4 - 4, y4 + 8))),
    )
    hi, lo = zy_weights(coarse_taps, zi, yi, o >> 5, (o & 15) >> 1, 8)
    wc[0] = hi
    wc[1] = lo

    k, n = iota((384, 256), 0), iota((384, 256), 1)
    xo, v = n & 127, n >> 7
    w = jnp.where(
        k < 256,
        jnp.where((k >> 7) == v, taps_at(fine_taps, 2, (k & 127) - xo + 4), 0.0),
        jnp.where(((k >> 6) & 1) == v, taps_at(coarse_taps, 2, (k & 63) - (xo >> 1) + 4), 0.0),
    )
    hi, lo = hi_lo(w)
    xw[0] = hi
    xw[1] = lo
    r, n = iota((32, 256), 0), iota((32, 256), 1)
    xo, v, e = n & 127, n >> 7, r & 3
    right = r >= 16
    w = jnp.where(
        (r & 8) == 0,
        taps_at(fine_taps, 2, e + jnp.where(right, 128, -4) - xo + 4),
        taps_at(coarse_taps, 2, e + jnp.where(right, 64, -4) - (xo >> 1) + 4),
    )
    there = jnp.where(right, jnp.where(gx < NGX - 1, 1, 0), jnp.where(gx > 0, 1, 0)) == 1
    hi, lo = hi_lo(jnp.where(there & (((r >> 2) & 1) == v), w, 0.0))
    xh[pl.ds(0, 32)] = hi
    xh[pl.ds(32, 32)] = lo

    for cp in stage2:
        cp.wait()
    stage3 = []
    for d in range(1, NGX):
        cp = remote(gath.at[gx], gath.at[gx], s3s.at[d - 1], s3r.at[d - 1], dev(d, 0, 0))
        cp.start()
        stage3.append(cp)

    load_top.wait()
    k, n = iota((512, 512), 0), iota((512, 512), 1)
    target = (((k >> 4) & 3) << 7) + ((k >> 7) << 5) + (((k >> 6) & 1) << 4) + (k & 15)
    perm[...] = jnp.where(n == target, 1.0, 0.0).astype(BF16)

    def reorder(i, carry):
        parts = []
        for g in range(4):
            for half in range(2):
                pieces = [
                    kv[:, pl.ds(pl.multiple_of(((half * 4 + z4) * 16 + i * 4 + g) * 128, 128), 128)]
                    for z4 in range(4)
                ]
                parts.append(jnp.concatenate(pieces, axis=1))
        got = nn(jnp.concatenate(parts, axis=0), perm[...]).astype(BF16)
        for g in range(8):
            at = pl.ds(pl.multiple_of((i * 8 + g) * 128, 128), 128)
            for x in range(4):
                kp[x, :, at] = got[g * 64 : g * 64 + 64, x * 128 : x * 128 + 128]
        return carry

    lax.fori_loop(0, 4, reorder, 0)

    r, c = iota((32, 384), 0), iota((32, 384), 1)
    t, e, right = (r >> 2) & 3, r & 3, r >= 16
    spot = jnp.where(
        t < 2, t * 128 + jnp.where(right, 124, 0), 256 + (t & 1) * 64 + jnp.where(right, 60, 0)
    )
    pick = jnp.where(c == spot + e, 1.0, 0.0).astype(BF16)

    def zy_pass(p, carry):
        pair = jnp.concatenate([fld[2 * p], fld[2 * p + 1]], axis=1)
        near = jnp.concatenate([halo[2 * p], halo[2 * p + 1]], axis=1)
        got = (
            nn(wf[0, :, pl.ds(0, 256)], pair) + nn(wf[0, :, pl.ds(256, 320)], near)
            + nn(wf[1, :, pl.ds(0, 256)], pair) + nn(wf[1, :, pl.ds(256, 320)], near)
        )
        cells = jnp.concatenate([cl[p].reshape(64, 128), ch[p].reshape(192, 128)], axis=0)
        got_coarse = nn(wc[0], cells) + nn(wc[1], cells)
        both = jnp.concatenate([got.astype(BF16), got_coarse.astype(BF16)], axis=1)
        tt[p] = both
        ends = nt(pick, both).astype(BF16)
        edge_out[0, p] = ends[:16]
        edge_out[1, p] = ends[16:]
        return carry

    edges = []
    for cp in coarse:
        cp.wait()
    for h in range(NCH):
        for cp in fine[h]:
            cp.wait()
        lax.fori_loop(h * PCH, (h + 1) * PCH, zy_pass, 0, unroll=2)
        ps = pl.ds(h * PCH, PCH)
        left = remote(edge_out.at[0, ps], edge_in.at[1, ps], es.at[h, 0], er.at[h, 0], dev(-1, 0, 0))
        right = remote(edge_out.at[1, ps], edge_in.at[0, ps], es.at[h, 1], er.at[h, 1], dev(1, 0, 0))
        left.start()
        right.start()
        edges.append((left, right))

    def x_pass(p, carry):
        both = tt[p]
        ends = jnp.concatenate([edge_in[0, p], edge_in[1, p]], axis=0)
        base[p] = nn(both, xw[0]) + nn(both, xw[1]) + tn(jnp.concatenate([ends, ends], axis=0), xh[...])
        return carry

    for h in range(NCH):
        for cp in edges[h]:
            cp.wait()
        lax.fori_loop(h * PCH, (h + 1) * PCH, x_pass, 0, unroll=2)

    def gather_dot(x):
        tiles = [gath[x, g, half] for g in range(NGY) for half in range(2)]
        return nt(kp[x], jnp.concatenate(tiles, axis=1))

    sums = gather_dot(gx)
    for d in range(1, NGX):
        stage3[d - 1].wait()
        sums = sums + gather_dot(lax.rem(gx + (NGX - d), NGX))

    k, n = iota((64, 512), 0), iota((64, 512), 1)
    spread = jnp.where(k == ((n >> 7) << 4) + ((n & 127) >> 3), 1.0, 0.0).astype(BF16)
    hi, lo = hi_lo(sums)
    lo2 = (sums - hi.astype(F32) - lo.astype(F32)).astype(BF16)
    prol[...] = tn(hi, spread) + tn(lo, spread) + tn(lo2, spread)

    def finish(p, carry):
        for v in range(2):
            for zt in range(2):
                rows = [
                    prol[pl.ds(2 * p + v, 1), pl.ds((zt * 2 + yt) * 128, 128)] for yt in range(2)
                ]
                block = jnp.concatenate([jnp.broadcast_to(row, (8, 128)) for row in rows], axis=0)
                for i in range(8):
                    at = pl.ds((zt * 8 + i) * 16, 16)
                    out[2 * p + v, at] = (base[p, at, pl.ds(v * 128, 128)] + block).astype(BF16)
        return carry

    lax.fori_loop(0, 8, finish, 0, unroll=True)


def shards(field, fine_taps, coarse_taps, top_kernel):
    vm = pltpu.VMEM
    dma = pltpu.SemaphoreType.DMA
    hbm = pl.BlockSpec(memory_space=pltpu.HBM)
    operands = [field.reshape(16, 256, 128), fine_taps, coarse_taps, top_kernel.reshape(64, 16384)]
    operands = [pltpu.with_memory_space_constraint(a, pltpu.HBM) for a in operands]
    out = pl.pallas_call(
        kernel,
        name="covariance",
        out_shape=pltpu.VMEM((16, 256, 128), BF16),
        in_specs=[hbm, hbm, hbm, hbm],
        out_specs=pl.BlockSpec(memory_space=pltpu.VMEM),
        scratch_shapes=[
            pltpu.SMEM((3, 9), F32),
            pltpu.SMEM((3, 9), F32),
            vm((16, 256, 128), BF16),
            vm((16, 320, 128), BF16),
            vm((2, 16, 64, 128), BF16),
            vm((8, 2, 2, 16, 128), BF16),
            vm((8, 12, 16, 128), BF16),
            vm((8, 256, 384), BF16),
            vm((2, 8, 16, 256), BF16),
            vm((2, 8, 16, 256), BF16),
            vm((8, 256, 256), F32),
            vm((2, 256, 576), BF16),
            vm((2, 256, 256), BF16),
            vm((2, 384, 256), BF16),
            vm((64, 256), BF16),
            vm((192, 256), BF16),
            vm((512, 128), BF16),
            vm((512, 512), BF16),
            vm((64, 16384), BF16),
            vm((4, 64, 4096), BF16),
            vm((4, 16, 2, 16, 128), BF16),
            vm((4, 16, 128), BF16),
            vm((16, 512), F32),
            vm((16, 512), F32),
            dma((NCH, 8)), dma((NCH, 8)),
            dma((8,)), dma((8,)),
            dma((NCH, 2)), dma((NCH, 2)),
            dma((3,)), dma((3,)),
            dma((15,)), dma((15,)),
            dma((3,)), dma((3,)),
            dma((4,)),
        ],
        compiler_params=pltpu.CompilerParams(
            collective_id=1, has_side_effects=True, vmem_limit_bytes=40 << 20
        ),
    )(*operands)
    return out.reshape(field.shape)


def solution(mesh):
    return jax.shard_map(
        shards,
        mesh=mesh,
        in_specs=(P(None, "gz", "gy", "gx"), P(), P(), P("gz", "gy", "gx", None)),
        out_specs=P(None, "gz", "gy", "gx"),
        check_vma=False,
    )
```

```python
import functools

import jax
import jax.numpy as jnp
from jax import lax
from jax.experimental import pallas as pl
from jax.experimental.pallas import tpu as pltpu
from jax.sharding import PartitionSpec as P

F32 = jnp.float32
BF16 = jnp.bfloat16
MESH = pl.DeviceIdType.MESH
NGX, NGY, NGZ = 4, 16, 4
NCH = 4
VCH = 16 // NCH
PCH = 8 // NCH


def iota(shape, dim):
    return lax.broadcasted_iota(jnp.int32, shape, dim)


def nn(a, b):
    return lax.dot_general(a, b, (((1,), (0,)), ((), ())), preferred_element_type=F32)


def nt(a, b):
    return lax.dot_general(a, b, (((1,), (1,)), ((), ())), preferred_element_type=F32)


def tn(a, b):
    return lax.dot_general(a, b, (((0,), (0,)), ((), ())), preferred_element_type=F32)


def hi_lo(w):
    hi = w.astype(BF16)
    return hi, (w - hi.astype(F32)).astype(BF16)


def taps_at(taps_ref, row, offset):
    value = jnp.zeros(offset.shape, F32)
    for k in range(9):
        value = jnp.where(offset == k, taps_ref[row, k], value)
    return value


def kernel(
    field, fine_hbm, coarse_hbm, top, out,
    fine_taps, coarse_taps,
    fld, halo, strips, cl, ch, tt, edge_out, edge_in, relay,
    wf, wc, xw, xh, gsel, rx, perm, kv, kp, gath, tile_in, psum, prol,
    fs, fr, cs, cr, es, er, s1s, s1r, s2s, s2r, s3s, s3r, lsem,
):
    gx, gy, gz = lax.axis_index("gx"), lax.axis_index("gy"), lax.axis_index("gz")

    def dev(dx, dy, dz):
        return (
            lax.rem(gx + (dx + NGX), NGX),
            lax.rem(gy + (dy + NGY), NGY),
            lax.rem(gz + (dz + NGZ), NGZ),
        )

    def remote(src, dst, ssem, rsem, to):
        return pltpu.make_async_remote_copy(
            src_ref=src, dst_ref=dst, send_sem=ssem, recv_sem=rsem, device_id=to, device_id_type=MESH
        )

    load_field = pltpu.make_async_copy(field, fld, lsem.at[0])
    load_top = pltpu.make_async_copy(top, kv, lsem.at[1])
    load_fine = pltpu.make_async_copy(fine_hbm, fine_taps, lsem.at[2])
    load_coarse = pltpu.make_async_copy(coarse_hbm, coarse_taps, lsem.at[3])
    load_field.start()
    load_fine.start()
    load_coarse.start()
    load_top.start()

    barrier = pltpu.get_barrier_semaphore()
    partners = [(i, 0, 0) for i in range(1, NGX)] + [(0, i, 0) for i in range(1, NGY)]
    partners += [(0, 0, i) for i in range(1, NGZ)]
    for d in partners:
        pl.semaphore_signal(barrier, inc=1, device_id=dev(*d), device_id_type=MESH)

    r, c = iota((192, 256), 0), iota((192, 256), 1)
    z, y = c >> 4, c & 15
    strip_z, strip_y = (r & 63) >> 2, (r & 3) + jnp.where(r >= 64, 12, 0)
    q = r - 128
    cz, cy = ((q >> 5) << 2) + ((q >> 2) & 3), (((q >> 4) & 1) << 2) + (q & 3)
    is_strip = (z == strip_z) & (y == strip_y)
    is_mean = ((z >> 1) == cz) & ((y >> 1) == cy)
    gsel[...] = jnp.where(
        r < 128, jnp.where(is_strip, 1.0, 0.0), jnp.where(is_mean, 0.25, 0.0)
    ).astype(BF16)
    r, c = iota((64, 128), 0), iota((64, 128), 1)
    spot = (((r >> 4) & 1) << 6) + (((r >> 2) & 3) << 4) + (r & 3) + jnp.where(r >= 32, 12, 0)
    rsel = jnp.where(c == spot, 1.0, 0.0).astype(BF16)
    k, n = iota((512, 128), 0), iota((512, 128), 1)
    rx[...] = jnp.where(((k >> 8) == (n >> 6)) & (((k & 127) >> 1) == (n & 63)), 0.5, 0.0).astype(BF16)

    load_fine.wait()
    load_coarse.wait()
    zmin, zmax = jnp.where(gz > 0, -99, 0), jnp.where(gz < NGZ - 1, 99, 0)
    ymin, ymax = jnp.where(gy > 0, -99, 0), jnp.where(gy < NGY - 1, 99, 0)

    def spread_taps(taps_ref, row, low, high, target, source):
        r, k = iota((16, 32), 0), iota((16, 32), 1)
        ok = (k - 4 >= low) & (k - 4 < high)
        table = jnp.where(ok, taps_at(taps_ref, row, k - r), 0.0)
        hi, lo = hi_lo(table)
        lo2 = (table - hi.astype(F32) - lo.astype(F32)).astype(BF16)
        k = iota((32, source.shape[1]), 0)
        columns = jnp.where(k == source + 4, 1.0, 0.0).astype(BF16)
        k = iota((256, 48), 1)
        rows = jnp.where((k & 15) == target, 1.0, 0.0).astype(BF16)
        return nn(rows, nn(jnp.concatenate([hi, lo, lo2], axis=0), columns).astype(BF16))

    o = iota((256, 48), 0)
    c = iota((32, 576), 1)
    near = c - 256
    z4, y4, q = (c >> 2) & 3, c & 3, (c >> 4) & 3
    zi = jnp.where(
        c < 256, c >> 4,
        jnp.where(
            near < 64, (near >> 4) - 4,
            jnp.where(near < 128, (near >> 4) + 12, jnp.where(near < 256, (near & 63) >> 2, jnp.where((q & 1) == 0, z4 - 4, z4 + 16))),
        ),
    )
    yi = jnp.where(
        near < 128, c & 15,
        jnp.where(near < 192, y4 - 4, jnp.where(near < 256, y4 + 16, jnp.where(q < 2, y4 - 4, y4 + 16))),
    )
    hi, lo = hi_lo(
        spread_taps(fine_taps, 0, zmin, zmax + 16, o >> 4, zi)
        * spread_taps(fine_taps, 1, ymin, ymax + 16, o & 15, yi)
    )
    wf[0] = hi
    wf[1] = lo
    c = iota((32, 256), 1)
    z4, y4, q = (c >> 2) & 3, c & 3, c >> 4
    first = (q & 1) * 4
    zi = jnp.where(
        q < 4, ((q >> 1) << 2) + z4,
        jnp.where(q < 6, z4 - 4, jnp.where(q < 8, z4 + 8, jnp.where(q < 12, first + z4, jnp.where((q & 1) == 0, z4 - 4, z4 + 8)))),
    )
    yi = jnp.where(
        q < 8, first + y4,
        jnp.where(q < 10, y4 - 4, jnp.where(q < 12, y4 + 8, jnp.where(q < 14, y4 - 4, y4 + 8))),
    )
    hi, lo = hi_lo(
        spread_taps(coarse_taps, 0, zmin, zmax + 8, o >> 5, zi)
        * spread_taps(coarse_taps, 1, ymin, ymax + 8, (o & 15) >> 1, yi)
    )
    wc[0] = hi
    wc[1] = lo

    k, n = iota((128, 128), 0), iota((128, 128), 1)
    fine_parts = hi_lo(taps_at(fine_taps, 2, k - n + 4))
    k, n = iota((64, 128), 0), iota((64, 128), 1)
    coarse_parts = hi_lo(taps_at(coarse_taps, 2, k - (n >> 1) + 4))
    for part in range(2):
        for v in range(2):
            own, other = pl.ds(v * 128, 128), pl.ds(128 - v * 128, 128)
            xw[part, pl.ds(v * 128, 128), own] = fine_parts[part]
            xw[part, pl.ds(v * 128, 128), other] = jnp.zeros((128, 128), BF16)
            xw[part, pl.ds(256 + v * 64, 64), own] = coarse_parts[part]
            xw[part, pl.ds(256 + v * 64, 64), other] = jnp.zeros((64, 128), BF16)
    r, n = iota((32, 256), 0), iota((32, 256), 1)
    xo, v, e = n & 127, n >> 7, r & 3
    right = r >= 16
    w = jnp.where(
        (r & 8) == 0,
        taps_at(fine_taps, 2, e + jnp.where(right, 128, -4) - xo + 4),
        taps_at(coarse_taps, 2, e + jnp.where(right, 64, -4) - (xo >> 1) + 4),
    )
    there = jnp.where(right, jnp.where(gx < NGX - 1, 1, 0), jnp.where(gx > 0, 1, 0)) == 1
    hi, lo = hi_lo(jnp.where(there & (((r >> 2) & 1) == v), w, 0.0))
    xh[pl.ds(0, 32)] = hi
    xh[pl.ds(32, 32)] = lo
    r, c = iota((32, 384), 0), iota((32, 384), 1)
    t, e, right = (r >> 2) & 3, r & 3, r >= 16
    spot = jnp.where(
        t < 2, t * 128 + jnp.where(right, 124, 0), 256 + (t & 1) * 64 + jnp.where(right, 60, 0)
    )
    pick = jnp.where(c == spot + e, 1.0, 0.0).astype(BF16)

    load_field.wait()
    r, c = iota((32, 256), 0), iota((32, 256), 1)
    rows = jnp.where(((r & 15) == (c >> 4)) & (((c & 15) >> 3) == (r >> 4)), 1.0, 0.0).astype(BF16)
    for zt in range(2):
        total = fld[:, pl.ds(zt * 128, 16), :].astype(F32)
        for i in range(1, 8):
            total = total + fld[:, pl.ds(zt * 128 + i * 16, 16), :].astype(F32)
        total = total.reshape(256, 128)
        hi, lo = hi_lo(total)
        lo2 = (total - hi.astype(F32) - lo.astype(F32)).astype(BF16)
        both = nn(rows, hi) + nn(rows, lo) + nn(rows, lo2)
        for yt in range(2):
            psum[:, pl.ds((zt * 2 + yt) * 128, 128)] = both[yt * 16 : yt * 16 + 16]
    k, n = iota((512, 128), 0), iota((512, 128), 1)
    spot = lax.rem(gz, 2) * 64 + ((k >> 7) << 4) + ((k & 127) >> 3)
    place = jnp.where(n == spot, 1.0 / 512.0, 0.0).astype(BF16)
    sums = psum[...]
    hi, lo = hi_lo(sums)
    lo2 = (sums - hi.astype(F32) - lo.astype(F32)).astype(BF16)
    tile_in[gz] = (nn(hi, place) + nn(lo, place) + nn(lo2, place)).astype(BF16)

    pl.semaphore_wait(barrier, len(partners))

    stage1 = []
    for d in range(1, NGZ):
        cp = remote(tile_in.at[gz], tile_in.at[gz], s1s.at[d - 1], s1r.at[d - 1], dev(0, 0, d))
        cp.start()
        stage1.append(cp)

    def fine_z(h, i):
        vs, dz = pl.ds(h * VCH, VCH), 1 - 2 * i
        src = fld.at[vs, pl.ds(192 - 192 * i, 64)]
        return remote(src, halo.at[vs, pl.ds(64 * i, 64)], fs.at[h, i], fr.at[h, i], dev(0, 0, dz))

    def fine_y(h, i):
        vs, dy = pl.ds(h * VCH, VCH), 1 - 2 * i
        dst = halo.at[vs, pl.ds(128 + 64 * i, 64)]
        return remote(strips.at[1 - i, vs], dst, fs.at[h, 2 + i], fr.at[h, 2 + i], dev(0, dy, 0))

    def fine_corner(h, i):
        vs, dy = pl.ds(h * VCH, VCH), 1 - 2 * i
        dst = halo.at[vs, pl.ds(256 + 32 * i, 32)]
        return remote(relay.at[1 - i, vs], dst, fs.at[h, 4 + i], fr.at[h, 4 + i], dev(0, dy, 0))

    def coarse_z(i):
        return remote(cl.at[:, 1 - i], ch.at[:, i], cs.at[i], cr.at[i], dev(0, 0, 1 - 2 * i))

    def coarse_y(i):
        return remote(cl.at[:, :, 1 - i], ch.at[:, 2 + i], cs.at[2 + i], cr.at[2 + i], dev(0, 1 - 2 * i, 0))

    def coarse_corner(i):
        src = ch.at[:, pl.ds(0, 2), 1 - i]
        return remote(src, ch.at[:, 4 + i], cs.at[4 + i], cr.at[4 + i], dev(0, 1 - 2 * i, 0))

    z_copies = [[fine_z(h, i) for i in range(2)] for h in range(NCH)]
    y_copies = [[fine_y(h, i) for i in range(2)] for h in range(NCH)]
    corner_copies = [[fine_corner(h, i) for i in range(2)] for h in range(NCH)]
    coarse_z_copies = [coarse_z(i) for i in range(2)]
    coarse_y_copies = [coarse_y(i) for i in range(2)]
    coarse_corner_copies = [coarse_corner(i) for i in range(2)]

    def start(copies):
        for cp in copies:
            cp.start()

    def wait(copies):
        for cp in copies:
            cp.wait()

    start(z_copies[0])
    start(z_copies[1])

    def cut(p, carry):
        pair = jnp.concatenate([fld[2 * p], fld[2 * p + 1]], axis=1)
        got = nn(gsel[...], pair)
        for v in range(2):
            for side in range(2):
                strips[side, 2 * p + v] = got[side * 64 : side * 64 + 64, v * 128 : v * 128 + 128].astype(BF16)
        means = got[128:192]
        hi, lo = hi_lo(means)
        both = jnp.concatenate([hi[:, :128], lo[:, :128], hi[:, 128:], lo[:, 128:]], axis=1)
        cl[p] = nn(both, rx[...]).astype(BF16).reshape(2, 2, 16, 128)
        return carry

    lax.fori_loop(0, 8, cut, 0, unroll=4)
    start(coarse_z_copies)
    start(z_copies[2])
    start(z_copies[3])
    start(coarse_y_copies)
    for h in range(NCH):
        start(y_copies[h])

    for cp in stage1:
        cp.wait()
    for half in range(2):
        gath[gx, gy, half] = tile_in[2 * half] + tile_in[2 * half + 1]
    stage2 = []
    for d in range(1, NGY):
        cp = remote(gath.at[gx, gy], gath.at[gx, gy], s2s.at[d - 1], s2r.at[d - 1], dev(0, d, 0))
        cp.start()
        stage2.append(cp)

    def forward(h):
        wait(z_copies[h])
        for p in range(h * PCH, (h + 1) * PCH):
            pair = [halo[2 * p + v, pl.ds(0, 128)] for v in range(2)]
            got = nn(rsel, jnp.concatenate(pair, axis=1)).astype(BF16)
            for v in range(2):
                for side in range(2):
                    relay[side, 2 * p + v] = got[side * 32 : side * 32 + 32, v * 128 : v * 128 + 128]
        start(corner_copies[h])

    forward(0)

    load_top.wait()
    k, n = iota((512, 512), 0), iota((512, 512), 1)
    target = (((k >> 4) & 3) << 7) + ((k >> 7) << 5) + (((k >> 6) & 1) << 4) + (k & 15)
    perm[...] = jnp.where(n == target, 1.0, 0.0).astype(BF16)

    def reorder(i, carry):
        parts = []
        for g in range(4):
            for half in range(2):
                pieces = [
                    kv[:, pl.ds(pl.multiple_of(((half * 4 + z4) * 16 + i * 4 + g) * 128, 128), 128)]
                    for z4 in range(4)
                ]
                parts.append(jnp.concatenate(pieces, axis=1))
        got = nn(jnp.concatenate(parts, axis=0), perm[...]).astype(BF16)
        for g in range(8):
            at = pl.ds(pl.multiple_of((i * 8 + g) * 128, 128), 128)
            for x in range(4):
                kp[x, :, at] = got[g * 64 : g * 64 + 64, x * 128 : x * 128 + 128]
        return carry

    lax.fori_loop(0, 4, reorder, 0)

    for cp in stage2:
        cp.wait()
    stage3 = []
    for d in range(1, NGX):
        cp = remote(gath.at[gx], gath.at[gx], s3s.at[d - 1], s3r.at[d - 1], dev(d, 0, 0))
        cp.start()
        stage3.append(cp)

    def zy_pass(p, carry):
        pair = jnp.concatenate([fld[2 * p], fld[2 * p + 1]], axis=1)
        near = jnp.concatenate([halo[2 * p], halo[2 * p + 1]], axis=1)
        got = (
            nn(wf[0, :, pl.ds(0, 256)], pair) + nn(wf[0, :, pl.ds(256, 320)], near)
            + nn(wf[1, :, pl.ds(0, 256)], pair) + nn(wf[1, :, pl.ds(256, 320)], near)
        )
        cells = jnp.concatenate([cl[p].reshape(64, 128), ch[p].reshape(192, 128)], axis=0)
        got_coarse = nn(wc[0], cells) + nn(wc[1], cells)
        both = jnp.concatenate([got.astype(BF16), got_coarse.astype(BF16)], axis=1)
        tt[p] = both
        ends = nt(pick, both).astype(BF16)
        edge_out[0, p] = ends[:16]
        edge_out[1, p] = ends[16:]
        return carry

    edges = []

    def zy_chunk(h):
        wait(y_copies[h])
        wait(corner_copies[h])
        for p in range(h * PCH, (h + 1) * PCH):
            zy_pass(p, 0)
        ps = pl.ds(h * PCH, PCH)
        left = remote(edge_out.at[0, ps], edge_in.at[1, ps], es.at[h, 0], er.at[h, 0], dev(-1, 0, 0))
        right = remote(edge_out.at[1, ps], edge_in.at[0, ps], es.at[h, 1], er.at[h, 1], dev(1, 0, 0))
        edges.append((left, right))
        start(edges[h])

    wait(coarse_z_copies)
    start(coarse_corner_copies)
    forward(1)
    wait(coarse_y_copies)
    wait(coarse_corner_copies)
    zy_chunk(0)
    forward(2)
    zy_chunk(1)
    forward(3)
    zy_chunk(2)
    zy_chunk(3)

    def gather_dot(x):
        tiles = [gath[x, g, half] for g in range(NGY) for half in range(2)]
        return nt(kp[x], jnp.concatenate(tiles, axis=1))

    sums = gather_dot(gx)
    for d in range(1, NGX):
        stage3[d - 1].wait()
        sums = sums + gather_dot(lax.rem(gx + (NGX - d), NGX))

    k, n = iota((64, 512), 0), iota((64, 512), 1)
    spread = jnp.where(k == ((n >> 7) << 4) + ((n & 127) >> 3), 1.0, 0.0).astype(BF16)
    hi, lo = hi_lo(sums)
    lo2 = (sums - hi.astype(F32) - lo.astype(F32)).astype(BF16)
    prol[...] = tn(hi, spread) + tn(lo, spread) + tn(lo2, spread)

    for h in range(NCH):
        wait(edges[h])
        for p in range(h * PCH, (h + 1) * PCH):
            both = tt[p]
            ends = jnp.concatenate([edge_in[0, p], edge_in[1, p]], axis=0)
            got = nn(both, xw[0]) + nn(both, xw[1]) + tn(jnp.concatenate([ends, ends], axis=0), xh[...])
            for v in range(2):
                for zt in range(2):
                    rows = [
                        prol[pl.ds(2 * p + v, 1), pl.ds((zt * 2 + yt) * 128, 128)] for yt in range(2)
                    ]
                    block = jnp.concatenate([jnp.broadcast_to(row, (8, 128)) for row in rows], axis=0)
                    block = jnp.concatenate([block] * 8, axis=0)
                    mine = got[zt * 128 : zt * 128 + 128, v * 128 : v * 128 + 128]
                    out[2 * p + v, pl.ds(zt * 128, 128)] = (mine + block).astype(BF16)


def shards(field, fine_taps, coarse_taps, top_kernel):
    vm = pltpu.VMEM
    dma = pltpu.SemaphoreType.DMA
    hbm = pl.BlockSpec(memory_space=pltpu.HBM)
    operands = [field.reshape(16, 256, 128), fine_taps, coarse_taps, top_kernel.reshape(64, 16384)]
    operands = [pltpu.with_memory_space_constraint(a, pltpu.HBM) for a in operands]
    out = pl.pallas_call(
        kernel,
        name="covariance",
        out_shape=pltpu.VMEM((16, 256, 128), BF16),
        in_specs=[hbm, hbm, hbm, hbm],
        out_specs=pl.BlockSpec(memory_space=pltpu.VMEM),
        scratch_shapes=[
            pltpu.SMEM((3, 9), F32),
            pltpu.SMEM((3, 9), F32),
            vm((16, 256, 128), BF16),
            vm((16, 320, 128), BF16),
            vm((2, 16, 64, 128), BF16),
            vm((8, 2, 2, 16, 128), BF16),
            vm((8, 6, 2, 16, 128), BF16),
            vm((8, 256, 384), BF16),
            vm((2, 8, 16, 256), BF16),
            vm((2, 8, 16, 256), BF16),
            vm((2, 16, 32, 128), BF16),
            vm((2, 256, 576), BF16),
            vm((2, 256, 256), BF16),
            vm((2, 384, 256), BF16),
            vm((64, 256), BF16),
            vm((192, 256), BF16),
            vm((512, 128), BF16),
            vm((512, 512), BF16),
            vm((64, 16384), BF16),
            vm((4, 64, 4096), BF16),
            vm((4, 16, 2, 16, 128), BF16),
            vm((4, 16, 128), BF16),
            vm((16, 512), F32),
            vm((16, 512), F32),
            dma((NCH, 6)), dma((NCH, 6)),
            dma((6,)), dma((6,)),
            dma((NCH, 2)), dma((NCH, 2)),
            dma((3,)), dma((3,)),
            dma((15,)), dma((15,)),
            dma((3,)), dma((3,)),
            dma((4,)),
        ],
        compiler_params=pltpu.CompilerParams(
            collective_id=1, has_side_effects=True, vmem_limit_bytes=40 << 20
        ),
    )(*operands)
    return out.reshape(field.shape)


def solution(mesh):
    return jax.shard_map(
        shards,
        mesh=mesh,
        in_specs=(P(None, "gz", "gy", "gx"), P(), P(), P("gz", "gy", "gx", None)),
        out_specs=P(None, "gz", "gy", "gx"),
        check_vma=False,
    )
```

```python
import functools

import jax
import jax.numpy as jnp
from jax import lax
from jax.experimental import pallas as pl
from jax.experimental.pallas import tpu as pltpu
from jax.sharding import PartitionSpec as P

F32 = jnp.float32
BF16 = jnp.bfloat16
MESH = pl.DeviceIdType.MESH
NGX, NGY, NGZ = 4, 16, 4
NCH = 4
VCH = 16 // NCH
PCH = 8 // NCH


def iota(shape, dim):
    return lax.broadcasted_iota(jnp.int32, shape, dim)


def nn(a, b):
    return lax.dot_general(a, b, (((1,), (0,)), ((), ())), preferred_element_type=F32)


def nt(a, b):
    return lax.dot_general(a, b, (((1,), (1,)), ((), ())), preferred_element_type=F32)


def tn(a, b):
    return lax.dot_general(a, b, (((0,), (0,)), ((), ())), preferred_element_type=F32)


def hi_lo(w):
    hi = w.astype(BF16)
    return hi, (w - hi.astype(F32)).astype(BF16)


def taps_at(taps_ref, row, offset):
    value = jnp.zeros(offset.shape, F32)
    for k in range(9):
        value = jnp.where(offset == k, taps_ref[row, k], value)
    return value


def kernel(
    field, fine_hbm, coarse_hbm, top, out,
    fine_taps, coarse_taps,
    fld, halo, strips, cl, ch, tt, edge_out, edge_in, relay,
    wf, wc, xw, xh, gsel, rx, perm, kv, kp, gath, tile_in, psum, prol,
    fs, fr, cs, cr, es, er, s1s, s1r, s2s, s2r, s3s, s3r, s4s, s4r, lsem,
):
    gx, gy, gz = lax.axis_index("gx"), lax.axis_index("gy"), lax.axis_index("gz")

    core = lax.rem(gy, 2)
    pair = lax.div(gy, 2)

    def dev(dx, dy, dz):
        return (
            lax.rem(gx + (dx + NGX), NGX),
            lax.rem(gy + (dy + NGY), NGY),
            lax.rem(gz + (dz + NGZ), NGZ),
        )

    def remote(src, dst, ssem, rsem, to):
        return pltpu.make_async_remote_copy(
            src_ref=src, dst_ref=dst, send_sem=ssem, recv_sem=rsem, device_id=to, device_id_type=MESH
        )

    load_field = pltpu.make_async_copy(field, fld, lsem.at[0])
    load_top = pltpu.make_async_copy(top, kv, lsem.at[1])
    load_fine = pltpu.make_async_copy(fine_hbm, fine_taps, lsem.at[2])
    load_coarse = pltpu.make_async_copy(coarse_hbm, coarse_taps, lsem.at[3])
    load_field.start()
    load_fine.start()
    load_coarse.start()
    load_top.start()

    barrier = pltpu.get_barrier_semaphore()
    partners = [(i, 0, 0) for i in range(1, NGX)] + [(0, i, 0) for i in (1, -1, *range(2, NGY, 2))]
    partners += [(0, 0, i) for i in range(1, NGZ)]
    for d in partners:
        pl.semaphore_signal(barrier, inc=1, device_id=dev(*d), device_id_type=MESH)

    r, c = iota((192, 256), 0), iota((192, 256), 1)
    z, y = c >> 4, c & 15
    strip_z, strip_y = (r & 63) >> 2, (r & 3) + jnp.where(r >= 64, 12, 0)
    q = r - 128
    cz, cy = ((q >> 5) << 2) + ((q >> 2) & 3), (((q >> 4) & 1) << 2) + (q & 3)
    is_strip = (z == strip_z) & (y == strip_y)
    is_mean = ((z >> 1) == cz) & ((y >> 1) == cy)
    gsel[...] = jnp.where(
        r < 128, jnp.where(is_strip, 1.0, 0.0), jnp.where(is_mean, 0.25, 0.0)
    ).astype(BF16)
    r, c = iota((64, 128), 0), iota((64, 128), 1)
    spot = (((r >> 4) & 1) << 6) + (((r >> 2) & 3) << 4) + (r & 3) + jnp.where(r >= 32, 12, 0)
    rsel = jnp.where(c == spot, 1.0, 0.0).astype(BF16)
    k, n = iota((512, 128), 0), iota((512, 128), 1)
    rx[...] = jnp.where(((k >> 8) == (n >> 6)) & (((k & 127) >> 1) == (n & 63)), 0.5, 0.0).astype(BF16)

    load_fine.wait()
    load_coarse.wait()
    zmin, zmax = jnp.where(gz > 0, -99, 0), jnp.where(gz < NGZ - 1, 99, 0)
    ymin, ymax = jnp.where(gy > 0, -99, 0), jnp.where(gy < NGY - 1, 99, 0)

    def spread_taps(taps_ref, row, low, high, target, source):
        r, k = iota((16, 32), 0), iota((16, 32), 1)
        ok = (k - 4 >= low) & (k - 4 < high)
        table = jnp.where(ok, taps_at(taps_ref, row, k - r), 0.0)
        hi, lo = hi_lo(table)
        lo2 = (table - hi.astype(F32) - lo.astype(F32)).astype(BF16)
        k = iota((32, source.shape[1]), 0)
        columns = jnp.where(k == source + 4, 1.0, 0.0).astype(BF16)
        k = iota((256, 48), 1)
        rows = jnp.where((k & 15) == target, 1.0, 0.0).astype(BF16)
        return nn(rows, nn(jnp.concatenate([hi, lo, lo2], axis=0), columns).astype(BF16))

    o = iota((256, 48), 0)
    c = iota((32, 576), 1)
    near = c - 256
    z4, y4, q = (c >> 2) & 3, c & 3, (c >> 4) & 3
    zi = jnp.where(
        c < 256, c >> 4,
        jnp.where(
            near < 64, (near >> 4) - 4,
            jnp.where(near < 128, (near >> 4) + 12, jnp.where(near < 256, (near & 63) >> 2, jnp.where((q & 1) == 0, z4 - 4, z4 + 16))),
        ),
    )
    yi = jnp.where(
        near < 128, c & 15,
        jnp.where(near < 192, y4 - 4, jnp.where(near < 256, y4 + 16, jnp.where(q < 2, y4 - 4, y4 + 16))),
    )
    hi, lo = hi_lo(
        spread_taps(fine_taps, 0, zmin, zmax + 16, o >> 4, zi)
        * spread_taps(fine_taps, 1, ymin, ymax + 16, o & 15, yi)
    )
    wf[0] = hi
    wf[1] = lo
    c = iota((32, 256), 1)
    z4, y4, q = (c >> 2) & 3, c & 3, c >> 4
    first = (q & 1) * 4
    zi = jnp.where(
        q < 4, ((q >> 1) << 2) + z4,
        jnp.where(q < 6, z4 - 4, jnp.where(q < 8, z4 + 8, jnp.where(q < 12, first + z4, jnp.where((q & 1) == 0, z4 - 4, z4 + 8)))),
    )
    yi = jnp.where(
        q < 8, first + y4,
        jnp.where(q < 10, y4 - 4, jnp.where(q < 12, y4 + 8, jnp.where(q < 14, y4 - 4, y4 + 8))),
    )
    hi, lo = hi_lo(
        spread_taps(coarse_taps, 0, zmin, zmax + 8, o >> 5, zi)
        * spread_taps(coarse_taps, 1, ymin, ymax + 8, (o & 15) >> 1, yi)
    )
    wc[0] = hi
    wc[1] = lo

    k, n = iota((128, 128), 0), iota((128, 128), 1)
    fine_parts = hi_lo(taps_at(fine_taps, 2, k - n + 4))
    k, n = iota((64, 128), 0), iota((64, 128), 1)
    coarse_parts = hi_lo(taps_at(coarse_taps, 2, k - (n >> 1) + 4))
    for part in range(2):
        for v in range(2):
            own, other = pl.ds(v * 128, 128), pl.ds(128 - v * 128, 128)
            xw[part, pl.ds(v * 128, 128), own] = fine_parts[part]
            xw[part, pl.ds(v * 128, 128), other] = jnp.zeros((128, 128), BF16)
            xw[part, pl.ds(256 + v * 64, 64), own] = coarse_parts[part]
            xw[part, pl.ds(256 + v * 64, 64), other] = jnp.zeros((64, 128), BF16)
    r, n = iota((32, 256), 0), iota((32, 256), 1)
    xo, v, e = n & 127, n >> 7, r & 3
    right = r >= 16
    w = jnp.where(
        (r & 8) == 0,
        taps_at(fine_taps, 2, e + jnp.where(right, 128, -4) - xo + 4),
        taps_at(coarse_taps, 2, e + jnp.where(right, 64, -4) - (xo >> 1) + 4),
    )
    there = jnp.where(right, jnp.where(gx < NGX - 1, 1, 0), jnp.where(gx > 0, 1, 0)) == 1
    hi, lo = hi_lo(jnp.where(there & (((r >> 2) & 1) == v), w, 0.0))
    xh[pl.ds(0, 32)] = hi
    xh[pl.ds(32, 32)] = lo
    r, c = iota((32, 384), 0), iota((32, 384), 1)
    t, e, right = (r >> 2) & 3, r & 3, r >= 16
    spot = jnp.where(
        t < 2, t * 128 + jnp.where(right, 124, 0), 256 + (t & 1) * 64 + jnp.where(right, 60, 0)
    )
    pick = jnp.where(c == spot + e, 1.0, 0.0).astype(BF16)

    load_field.wait()
    r, c = iota((32, 256), 0), iota((32, 256), 1)
    rows = jnp.where(((r & 15) == (c >> 4)) & (((c & 15) >> 3) == (r >> 4)), 1.0, 0.0).astype(BF16)
    for zt in range(2):
        total = fld[:, pl.ds(zt * 128, 16), :].astype(F32)
        for i in range(1, 8):
            total = total + fld[:, pl.ds(zt * 128 + i * 16, 16), :].astype(F32)
        total = total.reshape(256, 128)
        hi, lo = hi_lo(total)
        lo2 = (total - hi.astype(F32) - lo.astype(F32)).astype(BF16)
        both = nn(rows, hi) + nn(rows, lo) + nn(rows, lo2)
        for yt in range(2):
            psum[:, pl.ds((zt * 2 + yt) * 128, 128)] = both[yt * 16 : yt * 16 + 16]
    k, n = iota((512, 128), 0), iota((512, 128), 1)
    spot = lax.rem(gz, 2) * 64 + ((k >> 7) << 4) + ((k & 127) >> 3)
    place = jnp.where(n == spot, 1.0 / 512.0, 0.0).astype(BF16)
    sums = psum[...]
    hi, lo = hi_lo(sums)
    lo2 = (sums - hi.astype(F32) - lo.astype(F32)).astype(BF16)
    tile_in[gz] = (nn(hi, place) + nn(lo, place) + nn(lo2, place)).astype(BF16)

    pl.semaphore_wait(barrier, len(partners))

    stage1 = []
    for d in range(1, NGZ):
        cp = remote(tile_in.at[gz], tile_in.at[gz], s1s.at[d - 1], s1r.at[d - 1], dev(0, 0, d))
        cp.start()
        stage1.append(cp)

    def fine_z(h, i):
        vs, dz = pl.ds(h * VCH, VCH), 1 - 2 * i
        src = fld.at[vs, pl.ds(192 - 192 * i, 64)]
        return remote(src, halo.at[vs, pl.ds(64 * i, 64)], fs.at[h, i], fr.at[h, i], dev(0, 0, dz))

    def fine_y(h, i):
        vs, dy = pl.ds(h * VCH, VCH), 1 - 2 * i
        dst = halo.at[vs, pl.ds(128 + 64 * i, 64)]
        return remote(strips.at[1 - i, vs], dst, fs.at[h, 2 + i], fr.at[h, 2 + i], dev(0, dy, 0))

    def fine_corner(h, i):
        vs, dy = pl.ds(h * VCH, VCH), 1 - 2 * i
        dst = halo.at[vs, pl.ds(256 + 32 * i, 32)]
        return remote(relay.at[1 - i, vs], dst, fs.at[h, 4 + i], fr.at[h, 4 + i], dev(0, dy, 0))

    def coarse_z(i):
        return remote(cl.at[:, 1 - i], ch.at[:, i], cs.at[i], cr.at[i], dev(0, 0, 1 - 2 * i))

    def coarse_y(i):
        return remote(cl.at[:, :, 1 - i], ch.at[:, 2 + i], cs.at[2 + i], cr.at[2 + i], dev(0, 1 - 2 * i, 0))

    def coarse_corner(i):
        src = ch.at[:, pl.ds(0, 2), 1 - i]
        return remote(src, ch.at[:, 4 + i], cs.at[4 + i], cr.at[4 + i], dev(0, 1 - 2 * i, 0))

    z_copies = [[fine_z(h, i) for i in range(2)] for h in range(NCH)]
    y_copies = [[fine_y(h, i) for i in range(2)] for h in range(NCH)]
    corner_copies = [[fine_corner(h, i) for i in range(2)] for h in range(NCH)]
    coarse_z_copies = [coarse_z(i) for i in range(2)]
    coarse_y_copies = [coarse_y(i) for i in range(2)]
    coarse_corner_copies = [coarse_corner(i) for i in range(2)]

    def start(copies):
        for cp in copies:
            cp.start()

    def wait(copies):
        for cp in copies:
            cp.wait()

    start(z_copies[0])
    start(z_copies[1])

    def cut(p, carry):
        pair = jnp.concatenate([fld[2 * p], fld[2 * p + 1]], axis=1)
        got = nn(gsel[...], pair)
        for v in range(2):
            for side in range(2):
                strips[side, 2 * p + v] = got[side * 64 : side * 64 + 64, v * 128 : v * 128 + 128].astype(BF16)
        means = got[128:192]
        hi, lo = hi_lo(means)
        both = jnp.concatenate([hi[:, :128], lo[:, :128], hi[:, 128:], lo[:, 128:]], axis=1)
        cl[p] = nn(both, rx[...]).astype(BF16).reshape(2, 2, 16, 128)
        return carry

    lax.fori_loop(0, 8, cut, 0, unroll=4)
    start(coarse_z_copies)
    start(z_copies[2])
    start(z_copies[3])
    start(coarse_y_copies)
    start(y_copies[0])

    for cp in stage1:
        cp.wait()
    for half in range(2):
        gath[gx, pair, core, half] = tile_in[2 * half] + tile_in[2 * half + 1]
    stage2 = []
    for d in range(1, 8):
        mine = gath.at[gx, pair, core]
        cp = remote(mine, mine, s2s.at[d - 1], s2r.at[d - 1], dev(0, 2 * d, 0))
        cp.start()
        stage2.append(cp)

    for h in range(1, NCH):
        start(y_copies[h])

    def forward(h):
        wait(z_copies[h])
        for p in range(h * PCH, (h + 1) * PCH):
            pair = [halo[2 * p + v, pl.ds(0, 128)] for v in range(2)]
            got = nn(rsel, jnp.concatenate(pair, axis=1)).astype(BF16)
            for v in range(2):
                for side in range(2):
                    relay[side, 2 * p + v] = got[side * 32 : side * 32 + 32, v * 128 : v * 128 + 128]
        start(corner_copies[h])

    forward(0)

    load_top.wait()
    k, n = iota((512, 512), 0), iota((512, 512), 1)
    target = (((k >> 4) & 3) << 7) + ((k >> 7) << 5) + (((k >> 6) & 1) << 4) + (k & 15)
    perm[...] = jnp.where(n == target, 1.0, 0.0).astype(BF16)

    def reorder(i, carry):
        parts = []
        for g in range(4):
            for half in range(2):
                pieces = [
                    kv[:, pl.ds(pl.multiple_of(((half * 4 + z4) * 16 + i * 4 + g) * 128, 128), 128)]
                    for z4 in range(4)
                ]
                parts.append(jnp.concatenate(pieces, axis=1))
        got = nn(jnp.concatenate(parts, axis=0), perm[...]).astype(BF16)
        for g in range(8):
            at = pl.ds(pl.multiple_of((i * 8 + g) * 128, 128), 128)
            for x in range(4):
                kp[x, :, at] = got[g * 64 : g * 64 + 64, x * 128 : x * 128 + 128]
        return carry

    lax.fori_loop(0, 4, reorder, 0)

    def zy_pass(p, carry):
        pair = jnp.concatenate([fld[2 * p], fld[2 * p + 1]], axis=1)
        near = jnp.concatenate([halo[2 * p], halo[2 * p + 1]], axis=1)
        got = (
            nn(wf[0, :, pl.ds(0, 256)], pair) + nn(wf[0, :, pl.ds(256, 320)], near)
            + nn(wf[1, :, pl.ds(0, 256)], pair) + nn(wf[1, :, pl.ds(256, 320)], near)
        )
        cells = jnp.concatenate([cl[p].reshape(64, 128), ch[p].reshape(192, 128)], axis=0)
        got_coarse = nn(wc[0], cells) + nn(wc[1], cells)
        both = jnp.concatenate([got.astype(BF16), got_coarse.astype(BF16)], axis=1)
        tt[p] = both
        ends = nt(pick, both).astype(BF16)
        edge_out[0, p] = ends[:16]
        edge_out[1, p] = ends[16:]
        return carry

    edges = []

    def zy_chunk(h):
        wait(y_copies[h])
        wait(corner_copies[h])
        for p in range(h * PCH, (h + 1) * PCH):
            zy_pass(p, 0)
        ps = pl.ds(h * PCH, PCH)
        left = remote(edge_out.at[0, ps], edge_in.at[1, ps], es.at[h, 0], er.at[h, 0], dev(-1, 0, 0))
        right = remote(edge_out.at[1, ps], edge_in.at[0, ps], es.at[h, 1], er.at[h, 1], dev(1, 0, 0))
        edges.append((left, right))
        start(edges[h])

    wait(coarse_z_copies)
    start(coarse_corner_copies)
    for cp in stage2:
        cp.wait()
    stage3 = []
    for d in range(1, NGX):
        mine = gath.at[gx, :, core]
        cp = remote(mine, mine, s3s.at[d - 1], s3r.at[d - 1], dev(d, 0, 0))
        cp.start()
        stage3.append(cp)
    sibling = dev(0, 1 - 2 * core, 0)
    mine = gath.at[gx, :, core]
    shared = [remote(mine, mine, s4s.at[0], s4r.at[0], sibling)]
    shared[0].start()

    def share(d):
        stage3[d - 1].wait()
        theirs = gath.at[lax.rem(gx + (NGX - d), NGX), :, core]
        shared.append(remote(theirs, theirs, s4s.at[d], s4r.at[d], sibling))
        shared[d].start()

    forward(1)
    wait(coarse_y_copies)
    wait(coarse_corner_copies)
    zy_chunk(0)
    forward(2)
    zy_chunk(1)
    forward(3)
    for d in range(1, NGX):
        share(d)
    zy_chunk(2)
    zy_chunk(3)

    def gather_dot(x):
        tiles = [gath[x, g // 2, g % 2, half] for g in range(NGY) for half in range(2)]
        return nt(kp[x], jnp.concatenate(tiles, axis=1))

    shared[0].wait()
    sums = gather_dot(gx)
    for d in range(1, NGX):
        shared[d].wait()
        sums = sums + gather_dot(lax.rem(gx + (NGX - d), NGX))

    k, n = iota((64, 512), 0), iota((64, 512), 1)
    spread = jnp.where(k == ((n >> 7) << 4) + ((n & 127) >> 3), 1.0, 0.0).astype(BF16)
    hi, lo = hi_lo(sums)
    lo2 = (sums - hi.astype(F32) - lo.astype(F32)).astype(BF16)
    prol[...] = tn(hi, spread) + tn(lo, spread) + tn(lo2, spread)

    for h in range(NCH):
        wait(edges[h])
        for p in range(h * PCH, (h + 1) * PCH):
            both = tt[p]
            ends = jnp.concatenate([edge_in[0, p], edge_in[1, p]], axis=0)
            got = nn(both, xw[0]) + nn(both, xw[1]) + tn(jnp.concatenate([ends, ends], axis=0), xh[...])
            for v in range(2):
                for zt in range(2):
                    rows = [
                        prol[pl.ds(2 * p + v, 1), pl.ds((zt * 2 + yt) * 128, 128)] for yt in range(2)
                    ]
                    block = jnp.concatenate([jnp.broadcast_to(row, (8, 128)) for row in rows], axis=0)
                    block = jnp.concatenate([block] * 8, axis=0)
                    mine = got[zt * 128 : zt * 128 + 128, v * 128 : v * 128 + 128]
                    out[2 * p + v, pl.ds(zt * 128, 128)] = (mine + block).astype(BF16)


def shards(field, fine_taps, coarse_taps, top_kernel):
    vm = pltpu.VMEM
    dma = pltpu.SemaphoreType.DMA
    hbm = pl.BlockSpec(memory_space=pltpu.HBM)
    operands = [field.reshape(16, 256, 128), fine_taps, coarse_taps, top_kernel.reshape(64, 16384)]
    operands = [pltpu.with_memory_space_constraint(a, pltpu.HBM) for a in operands]
    out = pl.pallas_call(
        kernel,
        name="covariance",
        out_shape=pltpu.VMEM((16, 256, 128), BF16),
        in_specs=[hbm, hbm, hbm, hbm],
        out_specs=pl.BlockSpec(memory_space=pltpu.VMEM),
        scratch_shapes=[
            pltpu.SMEM((3, 9), F32),
            pltpu.SMEM((3, 9), F32),
            vm((16, 256, 128), BF16),
            vm((16, 320, 128), BF16),
            vm((2, 16, 64, 128), BF16),
            vm((8, 2, 2, 16, 128), BF16),
            vm((8, 6, 2, 16, 128), BF16),
            vm((8, 256, 384), BF16),
            vm((2, 8, 16, 256), BF16),
            vm((2, 8, 16, 256), BF16),
            vm((2, 16, 32, 128), BF16),
            vm((2, 256, 576), BF16),
            vm((2, 256, 256), BF16),
            vm((2, 384, 256), BF16),
            vm((64, 256), BF16),
            vm((192, 256), BF16),
            vm((512, 128), BF16),
            vm((512, 512), BF16),
            vm((64, 16384), BF16),
            vm((4, 64, 4096), BF16),
            vm((4, 8, 2, 2, 16, 128), BF16),
            vm((4, 16, 128), BF16),
            vm((16, 512), F32),
            vm((16, 512), F32),
            dma((NCH, 6)), dma((NCH, 6)),
            dma((6,)), dma((6,)),
            dma((NCH, 2)), dma((NCH, 2)),
            dma((3,)), dma((3,)),
            dma((7,)), dma((7,)),
            dma((3,)), dma((3,)),
            dma((4,)), dma((4,)),
            dma((4,)),
        ],
        compiler_params=pltpu.CompilerParams(
            collective_id=1, has_side_effects=True, vmem_limit_bytes=40 << 20
        ),
    )(*operands)
    return out.reshape(field.shape)


def solution(mesh):
    return jax.shard_map(
        shards,
        mesh=mesh,
        in_specs=(P(None, "gz", "gy", "gx"), P(), P(), P("gz", "gy", "gx", None)),
        out_specs=P(None, "gz", "gy", "gx"),
        check_vma=False,
    )
```
